512 devices in a mesh: row: 32 (over x, y), col: 16 (over z, core).
Axes of the slice: x: 4, y: 8, z: 8, core: 2. Of those that a mesh axis runs over, the one named last changes fastest.
Arguments:
- features: bfloat16 [131072, 128], P(('row', 'col')), may hold values from -6 to 6
- degree: int32 [131072], P(('row', 'col')), may hold values from 1 to 256
- weight: bfloat16 [128, 128], replicated, may hold values from -0.5 to 0.5
- bias: float32 [128], replicated, may hold values from -3 to 3
- cotangent: bfloat16 [131072, 128], P(('row', 'col')), may hold values from -8 to 8
- tile_rows: int32 [32, 16, 128], P('row', 'col'), may hold values from 0 to 31
- tile_cols: int32 [32, 16, 128], P('row', 'col'), may hold values from 0 to 63
- tile_count: int32 [32, 16, 1], P('row', 'col'), may hold values from 32 to 128, as said below
- tile_codes: int32 [32, 16, 128, 256], P('row', 'col'), may hold values from 0 to 4095
Outputs:
- hidden: bfloat16 [131072, 128], P(('row', 'col'))
- grad_features: bfloat16 [131072, 128], P(('row', 'col'))
- grad_weight: float32 [128, 128], replicated
- grad_bias: float32 [128], replicated
The draws below stay inside these ranges and needn't reach their ends.
Inputs may be any that keep to these rules, and one draw needn't show every extreme that they name: Only the first tile_count slots of a block are live; on some block the count is exactly 128. `tile_rows`: A tile position may repeat within a block; repeated tiles add.
All inputs are finite; a program needn't handle non-finite values.
Results may differ from the reference program's by a relative error of at most 0.019.
Values may be sent and summed in bfloat16 or wider, within the bound.
A program may use at most 64 MiB of HBM per device.

```python
import math
import jax
import jax.numpy as jnp
from jax import lax

FEAT = 128
TILE = 128
NODE_TILES = 2
SLOTS = 128
BLOCK = 16
ROW_TILES = 32
COL_TILES = 64
NODES = 131072
N_ROW = 32
N_COL = 16


def draw_cotangent(key, part):
    piece_rows = TILE * NODE_TILES
    piece_total = NODES // piece_rows
    piece_ids = jnp.arange(NODES, dtype=jnp.int32) // piece_rows
    ramp = 0.5 + piece_ids.astype(jnp.float32) / (piece_total - 1)
    noise = jnp.clip(jax.random.normal(jax.random.fold_in(key, 13), (NODES, FEAT), jnp.float32), -4.0, 4.0)
    values = noise * ramp[:, None]
    return values.astype(jnp.bfloat16)


def draw_tile_count(key, part):
    rows_axis = COL_TILES // NODE_TILES
    cols_axis = ROW_TILES // NODE_TILES
    device_total = rows_axis * cols_axis
    counts = jax.random.randint(jax.random.fold_in(key, 21), (device_total,), SLOTS // 4, SLOTS + 1, jnp.int32)
    fullest = jax.random.randint(jax.random.fold_in(key, 22), (), 0, device_total, jnp.int32)
    counts = counts.at[fullest].set(SLOTS)
    return counts.reshape(rows_axis, cols_axis, 1)


def touch_ends(drawn, rng, low, largest):
    extent = drawn.shape
    place = [jax.random.randint(jax.random.fold_in(rng, axis), (), 0, extent[axis]) for axis in range(len(extent))]
    drawn = drawn.at[tuple(place)].set(low)
    longest = extent.index(max(extent))
    place[longest] = (place[longest] + 1) % extent[longest]
    return drawn.at[tuple(place)].set(largest)


def shard_levels(stream_key, dims, cuts, low, top_value):
    def one(dim, shards_of):
        draws = jax.random.uniform(jax.random.fold_in(jax.random.fold_in(stream_key, 6), dim), (shards_of,), jnp.float32, low / len(cuts), top_value / len(cuts))
        return jnp.repeat(jnp.exp(draws), dims[dim] // shards_of).reshape((-1,) + (1,) * (len(dims) - dim - 1))

    factor_of = one(*cuts[0])
    for cut in cuts[1:]:
        factor_of = factor_of * one(*cut)
    return factor_of


def bell_draw(own_key, shape, scale, most, cuts=(), held_as=jnp.bfloat16):
    entries = jax.random.normal(own_key, shape, jnp.float32) * scale
    if len(cuts) > 0:
        entries = shard_levels(own_key, shape, cuts, -0.22, 0.18) * entries
    return jnp.clip(entries, min=-most, max=most).astype(held_as)


def setup_inputs(seed: int = 0) -> dict:
    keys = jax.random.split(jax.random.key(seed), 10)
    return {
        "features": bell_draw(keys[0], (NODES, FEAT), 1.0, 6.0, ((0, 512),)),
        "degree": touch_ends(jax.random.randint(keys[1], (NODES,), 1, 257), jax.random.fold_in(keys[1], 1), 1, 256).astype(jnp.int32),
        "weight": bell_draw(keys[2], (FEAT, FEAT), FEAT ** -0.5, 0.5),
        "bias": bell_draw(keys[3], (FEAT,), 0.5, 3.0, (), jnp.float32),
        "cotangent": draw_cotangent(jax.random.fold_in(keys[9], 71), 0),
        "tile_rows": touch_ends(jax.random.randint(keys[5], (N_ROW, N_COL, SLOTS), 0, ROW_TILES), jax.random.fold_in(keys[5], 1), 0, ROW_TILES - 1).astype(jnp.int32),
        "tile_cols": touch_ends(jax.random.randint(keys[6], (N_ROW, N_COL, SLOTS), 0, COL_TILES), jax.random.fold_in(keys[6], 1), 0, COL_TILES - 1).astype(jnp.int32),
        "tile_count": draw_tile_count(jax.random.fold_in(keys[9], 71), 0),
        "tile_codes": touch_ends(jax.random.randint(keys[8], (N_ROW, N_COL, SLOTS, 2 * TILE), 0, 4096), jax.random.fold_in(keys[8], 1), 0, 4095).astype(jnp.int32),
    }


def tile_mask(code_block, living):
    row_code = code_block[:, :TILE][:, :, None]
    col_code = code_block[:, TILE:][:, None, :]
    hashed = (row_code * col_code + row_code + 3 * col_code) % 4093
    return (hashed < 64) & living[:, None, None]

def device_sum(codes_dev, rows_dev, cols_dev, count_dev, source, out_tiles, backward):

    def block_step(summed, block_id):
        slot_start = block_id * BLOCK
        code_block = lax.dynamic_slice_in_dim(codes_dev, slot_start, BLOCK, 0)
        row_block = lax.dynamic_slice_in_dim(rows_dev, slot_start, BLOCK, 0)
        col_block = lax.dynamic_slice_in_dim(cols_dev, slot_start, BLOCK, 0)
        slot_ids = slot_start + jnp.arange(BLOCK, dtype=jnp.int32)
        living = slot_ids < count_dev
        keep = tile_mask(code_block, living).astype(jnp.float32)
        if backward:
            picked = source[row_block].astype(jnp.float32)
            product = jnp.einsum('tij,tif->tjf', keep, picked)
            return (summed.at[col_block].add(product), None)
        picked = source[col_block].astype(jnp.float32)
        product = jnp.einsum('tij,tjf->tif', keep, picked)
        return (summed.at[row_block].add(product), None)
    start_sum = jnp.zeros((out_tiles, TILE, FEAT), jnp.float32)
    summed, unused = lax.scan(block_step, start_sum, jnp.arange(SLOTS // BLOCK, dtype=jnp.int32))
    return summed

def reference(features, degree, weight, bias, cotangent, tile_rows, tile_cols, tile_count, tile_codes):
    pieces = TILE * NODE_TILES
    inv_root = lax.rsqrt(degree.astype(jnp.float32)).reshape(N_ROW, N_COL, pieces, 1)
    scaled = (inv_root * features.reshape(N_ROW, N_COL, pieces, FEAT).astype(jnp.float32)).astype(jnp.bfloat16)

    def forward_row(row_id):

        def add_col(col_id, summed):
            source = lax.dynamic_index_in_dim(scaled, col_id, 1, keepdims=False).reshape(COL_TILES, TILE, FEAT)
            partial_sum = device_sum(tile_codes[row_id, col_id], tile_rows[row_id, col_id], tile_cols[row_id, col_id], tile_count[row_id, col_id, 0], source, ROW_TILES, False)
            rounded = lax.optimization_barrier(partial_sum.astype(jnp.bfloat16))
            return summed + rounded.astype(jnp.float32)
        summed = lax.fori_loop(0, N_COL, add_col, jnp.zeros((ROW_TILES, TILE, FEAT), jnp.float32))
        row_root = lax.dynamic_index_in_dim(inv_root, row_id, 0, keepdims=False)
        return (row_root * summed.reshape(N_COL, pieces, FEAT)).astype(jnp.bfloat16)
    aggregate = lax.map(forward_row, jnp.arange(N_ROW, dtype=jnp.int32)).reshape(NODES, FEAT)
    preact = jnp.dot(aggregate, weight, preferred_element_type=jnp.float32) + bias
    hidden = jax.nn.elu(preact).astype(jnp.bfloat16)
    elu_slope = jnp.where(preact > 0, 1.0, jnp.exp(jnp.minimum(preact, 0.0)))
    grad_pre = cotangent.astype(jnp.float32) * elu_slope
    grad_pre_b = grad_pre.astype(jnp.bfloat16)
    grad_scale = 1.0 / math.sqrt(NODES)
    grad_weight = jnp.dot(aggregate.T, grad_pre_b, preferred_element_type=jnp.float32) * grad_scale
    grad_bias = lax.optimization_barrier(jnp.sum(grad_pre, axis=0)) * grad_scale
    grad_agg = jnp.dot(grad_pre_b, weight.T, preferred_element_type=jnp.float32)
    grad_scaled = (inv_root.reshape(NODES, 1) * grad_agg).astype(jnp.bfloat16).reshape(N_ROW, N_COL, pieces, FEAT)

    def backward_col(col_id):

        def add_row(row_id, summed):
            source = lax.dynamic_index_in_dim(grad_scaled, row_id, 0, keepdims=False).reshape(ROW_TILES, TILE, FEAT)
            partial_sum = device_sum(tile_codes[row_id, col_id], tile_rows[row_id, col_id], tile_cols[row_id, col_id], tile_count[row_id, col_id, 0], source, COL_TILES, True)
            rounded = lax.optimization_barrier(partial_sum.astype(jnp.bfloat16))
            return summed + rounded.astype(jnp.float32)
        summed = lax.fori_loop(0, N_ROW, add_row, jnp.zeros((COL_TILES, TILE, FEAT), jnp.float32))
        col_root = lax.dynamic_index_in_dim(inv_root, col_id, 1, keepdims=False)
        return (col_root * summed.reshape(N_ROW, pieces, FEAT)).astype(jnp.bfloat16)
    by_column = lax.map(backward_col, jnp.arange(N_COL, dtype=jnp.int32))
    grad_features = jnp.transpose(by_column, (1, 0, 2, 3)).reshape(NODES, FEAT)
    return (hidden, grad_features, grad_weight, grad_bias)
```

```python
import functools
import math

import jax
import jax.numpy as jnp
from jax import lax
from jax.experimental import pallas as pl
from jax.experimental.pallas import tpu as pltpu
from jax.sharding import PartitionSpec as P

MESH = pl.DeviceIdType.MESH
F32 = jnp.float32
BF16 = jnp.bfloat16
I32 = jnp.int32

NX, NY, NZ = 4, 8, 8
PIECE = 256
T = 128
SLOTS = 128
PRIME = 4093
ROUND = 12582912.0
CUT = 96

WIRE = 46e3
CORE_WIRE = 250e3
HOP = 1.7
CORE_HOP = 0.95


class Plan:
    def __init__(self):
        self.copies = {}
        self.actions = []
        self.fillers = []

    def message(self, key, link, nbytes, make):
        self.copies[key] = [link, nbytes, make, None]

    def action(self, deps, fn, sends=(), cost=0.03):
        self.actions.append((tuple(deps), fn, tuple(sends), cost))

    def filler(self, fn, cost):
        self.fillers.append((fn, cost))

    def run(self, leave=()):
        now = 0.0
        free = {}
        arrival = {}
        todo = list(self.actions)
        fill = list(self.fillers)
        waited = set()
        while todo:
            best, best_at = None, None
            for item in todo:
                if all(d in arrival for d in item[0]):
                    at = max([now] + [arrival[d] for d in item[0]])
                    if best is None or at < best_at - 1e-9:
                        best, best_at = item, at
            if fill and best_at > now + 0.1:
                fn, cost = fill.pop(0)
                fn()
                now += cost
                continue
            deps, fn, sends, cost = best
            todo.remove(best)
            for d in sorted(deps, key=lambda d: arrival[d]):
                if d not in waited:
                    waited.add(d)
                    self.copies[d][3].wait_recv()
            now = best_at
            if fn is not None:
                fn()
                now += cost
            for key in sends:
                link, nbytes, make, _ = self.copies[key]
                copy = make()
                self.copies[key][3] = copy
                copy.start()
                wire, hop = (CORE_WIRE, CORE_HOP) if link[0] == "c" else (WIRE, HOP)
                free[link] = max(free.get(link, 0.0), now) + nbytes / wire
                arrival[key] = free[link] + hop
        for fn, cost in fill:
            fn()
        for key, item in self.copies.items():
            if key not in waited and key not in leave:
                item[3].wait_recv()

    def drain(self):
        for item in self.copies.values():
            item[3].wait_send()


class Place:
    def __init__(self, send_sem, recv_sem):
        self.row = row = lax.axis_index("row")
        self.col = col = lax.axis_index("col")
        self.mx, self.my = row // NY, row % NY
        self.mz, self.core = col // 2, col % 2
        self.other = (row, self.mz * 2 + (1 - self.core))
        self.send_sem, self.recv_sem = send_sem, recv_sem
        self.used = 0

    def xy_piece(self, x, y):
        return lax.rem(self.mx + x + NX, NX) * NY + lax.rem(self.my + y + NY, NY)

    def z_piece(self, z, k):
        return lax.rem(self.mz + z + NZ, NZ) * 2 + k

    def at_xy(self, x, y):
        return (self.xy_piece(x, y), self.col)

    def at_z(self, z):
        return (self.row, self.z_piece(z, self.core))

    def copier(self, src, dst, dev):
        i = self.used
        self.used += 1

        def make():
            return pltpu.make_async_remote_copy(
                src_ref=src(), dst_ref=dst(), send_sem=self.send_sem.at[i], recv_sem=self.recv_sem.at[i],
                device_id=dev, device_id_type=MESH,
            )

        return make

    def enter(self, peers):
        barrier = pltpu.get_barrier_semaphore()
        for dev in peers:
            pl.semaphore_signal(barrier, inc=1, device_id=dev, device_id_type=MESH)

        def met():
            pl.semaphore_wait(barrier, len(peers))

        return met


def rows_of(start, first, size):
    return pl.ds(pl.multiple_of(start * PIECE + first, 16), size)


def tile_rows(t):
    return pl.ds(pl.multiple_of(t * T, T), T)


def slots_of(i, n):
    return pl.ds(pl.multiple_of(i * n, 8), n)


PARTS = {"A": (0, CUT), "B": (CUT, PIECE - CUT)}


def half(first, size, d):
    return (first, size // 2) if d > 0 else (first + size // 2, size // 2)


def part_rows(which, d, last):
    first, size = PARTS[which]
    return half(first, size, d) if last else (first, size)


def combine(dst, src, piece, first, size, given):
    whole = all(n >= size for _, _, _, n in given)
    blocks = [(first, size)] if whole else [half(first, size, 1), half(first, size, -1)]
    for f, n in blocks:
        v = src[rows_of(piece, f, n), :].astype(F32)
        for ref, base, gf, gn in given:
            if gf <= f and f + n <= gf + gn:
                v = v + ref[pl.ds(base + f - gf, n), :].astype(F32)
        dst[rows_of(piece, f, n), :] = v.astype(BF16)


def around(n):
    out = [n // 2]
    for k in range(n // 2 - 1, 0, -1):
        out += [k, -k]
    return out + [0]


COPIES1 = 76


def gather_body(
    feat_ref, deg_ref, rows_ref, cols_ref, count_ref, codes_ref,
    xg_ref, masks_ref, tab_ref,
    at_ref, b_ref, send_sem, recv_sem,
):
    me = Place(send_sem, recv_sem)
    met = me.enter([me.at_xy(1, 0), me.at_xy(-1, 0), me.at_xy(0, 1), me.at_xy(0, -1)])
    root = lax.rsqrt(deg_ref[...].astype(F32))
    for h in range(2):
        spread = jnp.broadcast_to(root[h : h + 1, :], (T, T)).T
        xg_ref[rows_of(me.row, h * T, T), :] = (spread * feat_ref[h * T : (h + 1) * T, :].astype(F32)).astype(BF16)
    met()
    plan = Plan()

    def leg(which, axis, o, d, k):
        n = NX if axis == "x" else NY
        first, size = part_rows(which, d, k == n // 2)
        back = -d * (k - 1)
        piece = me.xy_piece(back, o) if axis == "x" else me.xy_piece(o, back)
        where = lambda: xg_ref.at[rows_of(piece, first, size), :]
        dev = me.at_xy(d, 0) if axis == "x" else me.at_xy(0, d)
        key = (which, axis, o, d, k)
        plan.message(key, (axis, d), size * 256, me.copier(where, where, dev))
        return key

    for which, one, two in (("A", "x", "y"), ("B", "y", "x")):
        n1 = NX if one == "x" else NY
        n2 = NX if two == "x" else NY
        legs = {}
        for d in (1, -1):
            for k in range(1, n1 // 2 + 1):
                legs[d, k] = leg(which, one, 0, d, k)
        for d in (1, -1):
            plan.action([], None, [legs[d, 1]])
            for k in range(2, n1 // 2 + 1):
                plan.action([legs[d, k - 1]], None, [legs[d, k]])
        for o in range(-(n1 // 2) + 1, n1 // 2 + 1):
            if o == 0:
                need = []
            elif o == n1 // 2:
                need = [legs[1, o], legs[-1, o]]
            else:
                need = [legs[-1 if o > 0 else 1, abs(o)]]
            for d in (1, -1):
                before = need
                for k in range(1, n2 // 2 + 1):
                    key = leg(which, two, o, d, k)
                    plan.action(before, None, [key])
                    before = [key]

    def tables():
        lane = lax.broadcasted_iota(I32, (T, T), 1)
        sub = lax.broadcasted_iota(I32, (T, T), 0)
        out = []
        spread = [jnp.broadcast_to(v, (T, T)) for v in (rows_ref[...], cols_ref[...])]
        stood = [v.T for v in spread]
        for mine in (0, 1):
            key_l = spread[mine] * SLOTS + lane
            key_s = stood[mine] * SLOTS + sub
            rank = jnp.sum((key_s < key_l).astype(I32), axis=0, keepdims=True)
            hot = jnp.broadcast_to(rank, (T, T)).T == lane
            pick = lambda v: jnp.sum(jnp.where(hot, v, 0), axis=0, keepdims=True)
            order = pick(sub)
            target = pick(stood[mine])
            source = pick(stood[1 - mine])
            same = (target == pltpu.roll(target, 1, 1)) & (lane[:1] > 0)
            last = jnp.sum((stood[mine] <= lane).astype(I32), axis=0, keepdims=True) - 1
            has = jnp.sum((stood[mine] == lane).astype(I32), axis=0, keepdims=True)
            out += [order, source, same.astype(I32), jnp.maximum(last, 0), (has > 0).astype(I32)]
        for i, v in enumerate(out):
            tab_ref[i : i + 1, :] = v

    def codes_ready():
        live = lax.broadcasted_iota(I32, (SLOTS, T), 0) < count_ref[0, 0]
        a = codes_ref[:, :T] + 3
        a = jnp.where(a >= PRIME, a - PRIME, a)
        a = jnp.where(live, a, 0)
        at_ref[...] = a.astype(F32).T
        b = codes_ref[:, T:] + 1
        b_ref[...] = jnp.where(b >= PRIME, b - PRIME, b).astype(F32)

    def mask_group(g):
        at = at_ref[...]
        for u in range(8):
            s = g * 8 + u
            prod = at[:, u : u + 1] * b_ref[s : s + 1, :]
            near_q = (prod * (1.0 / PRIME) + ROUND) - ROUND
            left = prod - near_q * PRIME
            hit = (left >= 3.0) & (left < 67.0)
            masks_ref[s * T : (s + 1) * T, :] = jnp.where(hit, 1.0, 0.0).astype(BF16)
        at_ref[...] = pltpu.roll(at, T - 8, 1)

    plan.filler(codes_ready, 0.3)
    for g in range(SLOTS // 8):
        plan.filler(functools.partial(mask_group, g), 0.35)
    plan.filler(tables, 0.8)
    plan.run()
    plan.drain()


UNROLL = 8


def product_body(forward, tiles, tab_ref, masks_ref, src_ref, out_ref, pre_ref):
    base = 0 if forward else 5

    def step(g, acc):
        for u in range(UNROLL):
            j = g * UNROLL + u
            mask = masks_ref[tile_rows(tab_ref[base, j]), :]
            src = src_ref[tile_rows(tab_ref[base + 1, j]), :]
            new = jnp.dot(mask, src, preferred_element_type=F32) if forward else jnp.dot(src, mask, preferred_element_type=F32)
            acc = acc * tab_ref[base + 2, j].astype(F32) + new
            pre_ref[tile_rows(j), :] = acc
        return acc

    lax.fori_loop(0, SLOTS // UNROLL, step, jnp.zeros((T, T), F32))
    for t in range(tiles):
        v = pre_ref[tile_rows(tab_ref[base + 3, t]), :]
        out_ref[t * T : (t + 1) * T, :] = (v * tab_ref[base + 4, t].astype(F32)).astype(BF16)


COPIES2 = 40
W1 = T // 2
WZ = W1 // NZ


def dense_body(
    rp_ref, deg_ref, weight_ref, bias_ref, cot_ref,
    hid_ref, gt_ref, gsum_ref,
    acc_ref, cs_ref, zs_ref, gl_ref, g1_ref, gz_ref, g2_ref, send_sem, recv_sem,
):
    me = Place(send_sem, recv_sem)
    core, mz = me.core, me.mz
    met = me.enter([me.other] + [me.at_z(o) for o in range(1, NZ)])
    root = lax.rsqrt(deg_ref[...].astype(F32))
    met()
    plan = Plan()
    offsets = around(NZ)
    for i, o in enumerate(offsets):
        plan.message(
            ("c", o), ("c", 1), 65536,
            me.copier(
                functools.partial(lambda p: rp_ref.at[rows_of(p, 0, PIECE), :], me.z_piece(o, 1 - core)),
                functools.partial(lambda i: cs_ref.at[pl.ds(i * PIECE, PIECE), :], i),
                me.other,
            ),
        )
        plan.action([], None, [("c", o)], 0.05)
    legs = {}
    base = 0
    for d in (1, -1):
        for k in range(NZ // 2, 0, -1):
            first, size = (0, PIECE) if k < NZ // 2 else half(0, PIECE, d)
            piece = me.z_piece(d * k, core)
            legs[d, k] = (base, first, size, piece)
            plan.message(
                ("z", d, k), ("z", d), size * 256,
                me.copier(
                    functools.partial(lambda p, f, s: acc_ref.at[rows_of(p, f, s), :], piece, first, size),
                    functools.partial(lambda b, s: zs_ref.at[pl.ds(b, s), :], base, size),
                    me.at_z(d),
                ),
            )
            base += size

    def z_add(d, k):
        o = NZ // 2 if k == NZ // 2 else d * k
        _, first, size, piece = legs[d, k]
        given = [(cs_ref, offsets.index(o) * PIECE + first, first, size)]
        if k < NZ // 2:
            b, f, n, _ = legs[d, k + 1]
            given.append((zs_ref, b, f, n))
        combine(acc_ref, rp_ref, piece, first, size, given)

    for k in range(NZ // 2, 0, -1):
        for d in (1, -1):
            deps = [("c", NZ // 2 if k == NZ // 2 else d * k)]
            if k < NZ // 2:
                deps.append(("z", d, k + 1))
            plan.action(deps, functools.partial(z_add, d, k), [("z", d, k)], 0.08)
    plan.run()

    i0 = offsets.index(0)
    agg_sum = rp_ref[rows_of(me.col, 0, PIECE), :].astype(F32) + cs_ref[i0 * PIECE : (i0 + 1) * PIECE, :].astype(F32)
    for d in (1, -1):
        b = legs[d, 1][0]
        agg_sum = agg_sum + zs_ref[b : b + PIECE, :].astype(F32)
    spread = jnp.concatenate([jnp.broadcast_to(root[h : h + 1, :], (T, T)).T for h in range(2)], axis=0)
    aggregate = (spread * agg_sum).astype(BF16)
    weight = weight_ref[...]
    preact = jnp.dot(aggregate, weight, preferred_element_type=F32) + bias_ref[...]
    below = jnp.exp(jnp.minimum(preact, 0.0))
    hid_ref[...] = jnp.where(preact > 0, preact, below - 1.0).astype(BF16)
    grad_pre = cot_ref[...].astype(F32) * jnp.where(preact > 0, 1.0, below)
    grad_pre_b = grad_pre.astype(BF16)
    grad_agg_t = lax.dot_general(weight, grad_pre_b, (((1,), (1,)), ((), ())), preferred_element_type=F32)
    for h in range(2):
        gt_ref[rows_of(me.col, h * T, T), :] = (grad_agg_t[:, h * T : (h + 1) * T] * root[h : h + 1, :]).astype(BF16)

    plan2 = Plan()
    for d in (1, -1):
        for k in range(1, NZ // 2 + 1):
            first, size = (0, PIECE) if k < NZ // 2 else half(0, PIECE, d)
            piece = me.z_piece(-d * (k - 1), core)
            where = functools.partial(lambda p, f, s: gt_ref.at[rows_of(p, f, s), :], piece, first, size)
            plan2.message(("Z", d, k), ("z", d), size * 256, me.copier(where, where, me.at_z(d)))
    for o in offsets:
        where = functools.partial(lambda p: gt_ref.at[rows_of(p, 0, PIECE), :], me.z_piece(o, core))
        plan2.message(("C", o), ("c", 1), 65536, me.copier(where, where, me.other))
    plan2.action([], None, [("Z", 1, 1), ("Z", -1, 1), ("C", 0)])
    for d in (1, -1):
        for k in range(2, NZ // 2 + 1):
            plan2.action([("Z", d, k - 1)], None, [("Z", d, k)])
    for k in range(1, NZ // 2 + 1):
        if k == NZ // 2:
            plan2.action([("Z", 1, k), ("Z", -1, k)], None, [("C", k)])
        else:
            for d in (1, -1):
                plan2.action([("Z", d, k)], None, [("C", -d * k)])

    scale = 1.0 / math.sqrt(PIECE * NX * NY * NZ * 2)

    def grads():
        agg_t = aggregate.astype(F32).T.astype(BF16)
        gw = jnp.dot(agg_t, grad_pre_b, preferred_element_type=F32) * scale
        gb = jnp.sum(grad_pre, axis=0, keepdims=True) * scale
        gb8 = jnp.where(lax.broadcasted_iota(I32, (8, T), 0) == 0, gb, 0.0)
        for k in range(2):
            gl_ref[k * 72 : k * 72 + W1, :] = gw[k * W1 : (k + 1) * W1, :]
            gl_ref[k * 72 + W1 : (k + 1) * 72, :] = gb8

    plan2.message(
        ("G", 1), ("c", 1), 72 * 512,
        me.copier(lambda: gl_ref.at[slots_of(1 - core, 72), :], lambda: g1_ref.at[:, :], me.other),
    )
    plan2.action([], grads, [("G", 1)], 0.5)
    g2 = []
    for o in range(1, NZ):
        g2.append(("G2", o))
        plan2.message(
            ("G2", o), ("gz", o), 16 * 512,
            me.copier(
                functools.partial(lambda o: gz_ref.at[slots_of(lax.rem(mz + o, NZ), 16), :], o),
                lambda: g2_ref.at[slots_of(mz, 16), :],
                me.at_z(o),
            ),
        )

    def after_chip():
        total = gl_ref[slots_of(core, 72), :] + g1_ref[...]
        for z in range(NZ):
            gz_ref[z * 16 : z * 16 + 8, :] = total[z * WZ : (z + 1) * WZ, :]
            gz_ref[z * 16 + 8 : z * 16 + 16, :] = total[W1 : W1 + 8, :]
        g2_ref[slots_of(mz, 16), :] = gz_ref[slots_of(mz, 16), :]

    plan2.action([("G", 1)], after_chip, g2, 0.2)

    def after_z():
        gsum_ref[...] = total_of(g2_ref, NZ)

    plan2.action(g2, after_z, (), 0.1)
    plan2.run()
    plan.drain()
    plan2.drain()


def total_of(ref, n):
    v = ref[0:16, :]
    for i in range(1, n):
        v = v + ref[i * 16 : (i + 1) * 16, :]
    return v


COPIES3 = 76 + 3 + 7 + 7 + 1


def scatter_body(
    cp_ref, deg_ref, gsum_ref,
    gf_ref, gw_ref, gb_ref,
    acc_ref, sum_ref, g3_ref, g3x_ref, g4_ref, yx_ref, send_sem, recv_sem,
):
    me = Place(send_sem, recv_sem)
    core, mz, mx, my = me.core, me.mz, me.mx, me.my
    met = me.enter(
        [me.other]
        + [me.at_z(o) for o in range(1, NZ)]
        + [me.at_xy(o, 0) for o in range(1, NX)]
        + [me.at_xy(0, o) for o in range(1, NY)]
    )
    root = lax.rsqrt(deg_ref[...].astype(F32))
    met()
    plan = Plan()
    slot_rows = [0]

    def leg(which, axis, o, d, k, src):
        n = NX if axis == "x" else NY
        first, size = part_rows(which, d, k == n // 2)
        piece = me.xy_piece(d * k, o) if axis == "x" else me.xy_piece(o, d * k)
        base = slot_rows[0]
        slot_rows[0] += size
        dev = me.at_xy(d, 0) if axis == "x" else me.at_xy(0, d)
        key = ("s", which, axis, o, d, k)
        plan.message(
            key, (axis, d), size * 256,
            me.copier(
                lambda: src.at[rows_of(piece, first, size), :], lambda: sum_ref.at[pl.ds(base, size), :], dev
            ),
        )
        return dict(key=key, base=base, first=first, size=size, piece=piece)

    def given(*legs):
        return [(sum_ref, e["base"], e["first"], e["size"]) for e in legs]

    def adder(leg, *others):
        return lambda: combine(acc_ref, cp_ref, leg["piece"], leg["first"], leg["size"], given(*others))

    finals = {}
    late = []
    for which, one, two in (("A", "y", "x"), ("B", "x", "y")):
        n1 = NX if one == "x" else NY
        n2 = NX if two == "x" else NY
        done = {}
        for o in around(n2):
            ends = []
            for d in (1, -1):
                prev = None
                for k in range(n1 // 2, 0, -1):
                    now = leg(which, one, o, d, k, cp_ref if prev is None else acc_ref)
                    if prev is None:
                        plan.action([], None, [now["key"]])
                    else:
                        late.append(([prev["key"]], adder(now, prev), [now["key"]], 0.05))
                    prev = now
                ends.append(prev)
            done[o] = ends
        legs = {}
        for d in (1, -1):
            for k in range(n2 // 2, 0, -1):
                now = legs[d, k] = leg(which, two, 0, d, k, acc_ref)
                more = done[n2 // 2 if k == n2 // 2 else d * k] + ([legs[d, k + 1]] if k < n2 // 2 else [])
                late.append(([e["key"] for e in more], adder(now, *more), [now["key"]], 0.08))
        finals[which] = done[0] + [legs[1, 1], legs[-1, 1]]
    for deps, fn, sends, cost in late:
        plan.action(deps, fn, sends, cost)

    def ride(tag, n, dev, where, size):
        keys = []
        for o in range(1, n):
            keys.append((tag, o))
            plan.message((tag, o), (tag, o), size * 512, me.copier(where, where, dev(o)))
        return keys

    g3x = ride("G3x", NX, lambda o: me.at_xy(o, 0), lambda: g3x_ref.at[slots_of(mx, 16), :], 16)

    def start_x():
        g3x_ref[slots_of(mx, 16), :] = gsum_ref[...]

    plan.action([], start_x, g3x, 0.02)
    g3y = ride("G3y", NY, lambda o: me.at_xy(0, o), lambda: g3_ref.at[slots_of(my, 16), :], 16)

    def after_x():
        g3_ref[slots_of(my, 16), :] = total_of(g3x_ref, NX)

    plan.action(g3x, after_x, g3y, 0.05)
    own_w = lambda: pl.ds(pl.multiple_of(core * W1 + mz * WZ, 8), WZ)
    g4 = ride("G4", NZ, me.at_z, lambda: g4_ref.at[own_w(), :], WZ)

    def after_y():
        v = total_of(g3_ref, NY)
        gb_ref[...] = v[8:9, :]
        g4_ref[own_w(), :] = v[0:8, :]

    plan.action(g3y, after_y, g4, 0.05)
    half_w = lambda: g4_ref.at[slots_of(core, W1), :]
    plan.message(("G5", 0), ("c", 1), W1 * 512, me.copier(half_w, half_w, me.other))
    plan.action(g4, None, [("G5", 0)])

    def give_weight():
        gw_ref[...] = g4_ref[...]

    plan.action([("G5", 0)], give_weight, (), 0.05)
    plan.run()

    for which in ("A", "B"):
        first, size = PARTS[which]
        v = cp_ref[rows_of(me.row, first, size), :].astype(F32)
        for e in finals[which]:
            v = v + sum_ref[pl.ds(e["base"], e["size"]), :].astype(F32)
        yx_ref[first : first + size, :] = v
    for h in range(2):
        v = yx_ref[h * T : (h + 1) * T, :] * root[h : h + 1, :]
        gf_ref[h * T : (h + 1) * T, :] = v.T.astype(BF16)
    plan.drain()


VMEM = pl.BlockSpec(memory_space=pltpu.VMEM)
SMEM = pl.BlockSpec(memory_space=pltpu.SMEM)
ROW_NODES = PIECE * NZ * 2
COL_NODES = PIECE * NX * NY


def call(body, outs, ins, scratch, name, **params):
    return pl.pallas_call(
        body,
        out_shape=tuple(jax.ShapeDtypeStruct(*o) for o in outs),
        in_specs=ins,
        out_specs=(VMEM,) * len(outs),
        scratch_shapes=scratch,
        compiler_params=pltpu.CompilerParams(**params),
        name=name,
    )


def sems(n):
    return [pltpu.SemaphoreType.DMA((n,)), pltpu.SemaphoreType.DMA((n,))]


def local(features, degree, weight, bias, cotangent, tile_rows, tile_cols, tile_count, tile_codes):
    degree = degree.reshape(2, T)
    gather = call(
        gather_body,
        [((COL_NODES, T), BF16), ((SLOTS * T, T), BF16), ((16, T), I32)],
        [VMEM] * 4 + [SMEM, VMEM],
        [pltpu.VMEM((T, SLOTS), F32), pltpu.VMEM((SLOTS, T), F32)] + sems(COPIES1),
        "gather", collective_id=0, has_side_effects=True,
    )
    gathered, masks, table = gather(
        features, degree, tile_rows.reshape(1, SLOTS), tile_cols.reshape(1, SLOTS),
        tile_count.reshape(1, 1), tile_codes.reshape(SLOTS, 2 * T),
    )
    forward = call(
        functools.partial(product_body, True, ROW_NODES // T),
        [((ROW_NODES, T), BF16)],
        [SMEM, VMEM, VMEM],
        [pltpu.VMEM((SLOTS * T, T), F32)],
        "forward",
    )
    (row_terms,) = forward(table, masks, gathered)
    dense = call(
        dense_body,
        [((PIECE, T), BF16), ((ROW_NODES, T), BF16), ((16, T), F32)],
        [VMEM] * 5,
        [
            pltpu.VMEM((ROW_NODES, T), BF16),
            pltpu.VMEM((PIECE * NZ, T), BF16),
            pltpu.VMEM((PIECE * (NZ - 1), T), BF16),
            pltpu.VMEM((144, T), F32),
            pltpu.VMEM((72, T), F32),
            pltpu.VMEM((16 * NZ, T), F32),
            pltpu.VMEM((16 * NZ, T), F32),
        ]
        + sems(COPIES2),
        "dense", collective_id=1, has_side_effects=True,
    )
    hidden, grads_t, gsum = dense(row_terms, degree, weight, bias.reshape(1, T), cotangent)
    backward = call(
        functools.partial(product_body, False, COL_NODES // T),
        [((COL_NODES, T), BF16)],
        [SMEM, VMEM, VMEM],
        [pltpu.VMEM((SLOTS * T, T), F32)],
        "backward",
    )
    (col_terms,) = backward(table, masks, grads_t)
    scatter = call(
        scatter_body,
        [((PIECE, T), BF16), ((T, T), F32), ((1, T), F32)],
        [VMEM] * 3,
        [
            pltpu.VMEM((COL_NODES, T), BF16),
            pltpu.VMEM((COL_NODES - PIECE, T), BF16),
            pltpu.VMEM((16 * NY, T), F32),
            pltpu.VMEM((16 * NX, T), F32),
            pltpu.VMEM((T, T), F32),
            pltpu.VMEM((PIECE, T), F32),
        ]
        + sems(COPIES3),
        "scatter", collective_id=2, has_side_effects=True,
    )
    grad_features, grad_weight, grad_bias = scatter(col_terms, degree, gsum)
    return hidden, grad_features, grad_weight, grad_bias.reshape(T)


def solution(mesh):
    placed = (
        P(("row", "col"), None),
        P(("row", "col")),
        P(),
        P(),
        P(("row", "col"), None),
        P("row", "col", None),
        P("row", "col", None),
        P("row", "col", None),
        P("row", "col", None, None),
    )
    return jax.shard_map(
        local,
        mesh=mesh,
        in_specs=placed,
        out_specs=(P(("row", "col"), None), P(("row", "col"), None), P(), P()),
        check_vma=False,
    )
```

```python
import functools
import math

import jax
import jax.numpy as jnp
from jax import lax
from jax.experimental import pallas as pl
from jax.experimental.pallas import tpu as pltpu
from jax.sharding import PartitionSpec as P

MESH = pl.DeviceIdType.MESH
F32 = jnp.float32
BF16 = jnp.bfloat16
I32 = jnp.int32

NX, NY, NZ = 4, 8, 8
PIECE = 256
T = 128
SLOTS = 128
PRIME = 4093
ROUND = 12582912.0
CUT = 96

WIRE = 46e3
CORE_WIRE = 250e3
HOP = 1.7
CORE_HOP = 0.95


class Plan:
    def __init__(self):
        self.copies = {}
        self.actions = []
        self.fillers = []

    def message(self, key, link, nbytes, make):
        self.copies[key] = [link, nbytes, make, None]

    def action(self, deps, fn, sends=(), cost=0.03):
        self.actions.append((tuple(deps), fn, tuple(sends), cost))

    def filler(self, fn, cost):
        self.fillers.append((fn, cost))

    def run(self, leave=()):
        now = 0.0
        free = {}
        arrival = {}
        todo = list(self.actions)
        fill = list(self.fillers)
        waited = set()
        while todo:
            best, best_at = None, None
            for item in todo:
                if all(d in arrival for d in item[0]):
                    at = max([now] + [arrival[d] for d in item[0]])
                    if best is None or at < best_at - 1e-9:
                        best, best_at = item, at
            if fill and best_at > now + 0.1:
                fn, cost = fill.pop(0)
                fn()
                now += cost
                continue
            deps, fn, sends, cost = best
            todo.remove(best)
            for d in sorted(deps, key=lambda d: arrival[d]):
                if d not in waited:
                    waited.add(d)
                    self.copies[d][3].wait_recv()
            now = best_at
            if fn is not None:
                fn()
                now += cost
            for key in sends:
                link, nbytes, make, _ = self.copies[key]
                copy = make()
                self.copies[key][3] = copy
                copy.start()
                wire, hop = (CORE_WIRE, CORE_HOP) if link[0] == "c" else (WIRE, HOP)
                free[link] = max(free.get(link, 0.0), now) + nbytes / wire
                arrival[key] = free[link] + hop
        for fn, cost in fill:
            fn()
        for key, item in self.copies.items():
            if key not in waited and key not in leave:
                item[3].wait_recv()

    def drain(self):
        for item in self.copies.values():
            item[3].wait_send()


class Place:
    def __init__(self, send_sem, recv_sem):
        self.row = row = lax.axis_index("row")
        self.col = col = lax.axis_index("col")
        self.mx, self.my = row // NY, row % NY
        self.mz, self.core = col // 2, col % 2
        self.other = (row, self.mz * 2 + (1 - self.core))
        self.send_sem, self.recv_sem = send_sem, recv_sem
        self.used = 0

    def xy_piece(self, x, y):
        return lax.rem(self.mx + x + NX, NX) * NY + lax.rem(self.my + y + NY, NY)

    def z_piece(self, z, k):
        return lax.rem(self.mz + z + NZ, NZ) * 2 + k

    def at_xy(self, x, y):
        return (self.xy_piece(x, y), self.col)

    def at_z(self, z):
        return (self.row, self.z_piece(z, self.core))

    def copier(self, src, dst, dev):
        i = self.used
        self.used += 1

        def make():
            return pltpu.make_async_remote_copy(
                src_ref=src(), dst_ref=dst(), send_sem=self.send_sem.at[i], recv_sem=self.recv_sem.at[i],
                device_id=dev, device_id_type=MESH,
            )

        return make

    def enter(self, peers):
        barrier = pltpu.get_barrier_semaphore()
        for dev in peers:
            pl.semaphore_signal(barrier, inc=1, device_id=dev, device_id_type=MESH)

        def met():
            pl.semaphore_wait(barrier, len(peers))

        return met


def rows_of(start, first, size):
    return pl.ds(pl.multiple_of(start * PIECE + first, 16), size)


def tile_rows(t):
    return pl.ds(pl.multiple_of(t * T, T), T)


def slots_of(i, n):
    return pl.ds(pl.multiple_of(i * n, 8), n)


PARTS = {"A": (0, CUT), "B": (CUT, PIECE - CUT)}


def half(first, size, d):
    return (first, size // 2) if d > 0 else (first + size // 2, size // 2)


def part_rows(which, d, last):
    first, size = PARTS[which]
    return half(first, size, d) if last else (first, size)


def combine(dst, src, piece, first, size, given):
    whole = all(n >= size for _, _, _, n in given)
    blocks = [(first, size)] if whole else [half(first, size, 1), half(first, size, -1)]
    for f, n in blocks:
        v = src[rows_of(piece, f, n), :].astype(F32)
        for ref, base, gf, gn in given:
            if gf <= f and f + n <= gf + gn:
                v = v + ref[pl.ds(base + f - gf, n), :].astype(F32)
        dst[rows_of(piece, f, n), :] = v.astype(BF16)


def around(n):
    out = [n // 2]
    for k in range(n // 2 - 1, 0, -1):
        out += [k, -k]
    return out + [0]


def gather_part(me, root, met, feat_ref, rows_ref, cols_ref, count_ref, codes_ref, xg_ref, masks_ref, tab_ref, at_ref, b_ref):
    for h in range(2):
        spread = jnp.broadcast_to(root[h : h + 1, :], (T, T)).T
        xg_ref[rows_of(me.row, h * T, T), :] = (spread * feat_ref[h * T : (h + 1) * T, :].astype(F32)).astype(BF16)
    met()
    plan = Plan()

    def leg(which, axis, o, d, k):
        n = NX if axis == "x" else NY
        first, size = part_rows(which, d, k == n // 2)
        back = -d * (k - 1)
        piece = me.xy_piece(back, o) if axis == "x" else me.xy_piece(o, back)
        where = lambda: xg_ref.at[rows_of(piece, first, size), :]
        dev = me.at_xy(d, 0) if axis == "x" else me.at_xy(0, d)
        key = (which, axis, o, d, k)
        plan.message(key, (axis, d), size * 256, me.copier(where, where, dev))
        return key

    for which, one, two in (("A", "x", "y"), ("B", "y", "x")):
        n1 = NX if one == "x" else NY
        n2 = NX if two == "x" else NY
        legs = {}
        for d in (1, -1):
            for k in range(1, n1 // 2 + 1):
                legs[d, k] = leg(which, one, 0, d, k)
        for d in (1, -1):
            plan.action([], None, [legs[d, 1]])
            for k in range(2, n1 // 2 + 1):
                plan.action([legs[d, k - 1]], None, [legs[d, k]])
        for o in range(-(n1 // 2) + 1, n1 // 2 + 1):
            if o == 0:
                need = []
            elif o == n1 // 2:
                need = [legs[1, o], legs[-1, o]]
            else:
                need = [legs[-1 if o > 0 else 1, abs(o)]]
            for d in (1, -1):
                before = need
                for k in range(1, n2 // 2 + 1):
                    key = leg(which, two, o, d, k)
                    plan.action(before, None, [key])
                    before = [key]

    def tables():
        lane = lax.broadcasted_iota(I32, (T, T), 1)
        sub = lax.broadcasted_iota(I32, (T, T), 0)
        out = []
        spread = [jnp.broadcast_to(v, (T, T)) for v in (rows_ref[...], cols_ref[...])]
        stood = [v.T for v in spread]
        for mine in (0, 1):
            key_l = spread[mine] * SLOTS + lane
            key_s = stood[mine] * SLOTS + sub
            rank = jnp.sum((key_s < key_l).astype(I32), axis=0, keepdims=True)
            hot = jnp.broadcast_to(rank, (T, T)).T == lane
            pick = lambda v: jnp.sum(jnp.where(hot, v, 0), axis=0, keepdims=True)
            order = pick(sub)
            target = pick(stood[mine])
            source = pick(stood[1 - mine])
            same = (target == pltpu.roll(target, 1, 1)) & (lane[:1] > 0)
            last = jnp.sum((stood[mine] <= lane).astype(I32), axis=0, keepdims=True) - 1
            has = jnp.sum((stood[mine] == lane).astype(I32), axis=0, keepdims=True)
            out += [order, source, same.astype(I32), jnp.maximum(last, 0), (has > 0).astype(I32)]
        for i, v in enumerate(out):
            tab_ref[i : i + 1, :] = v

    def codes_ready():
        live = lax.broadcasted_iota(I32, (SLOTS, T), 0) < count_ref[0, 0]
        a = codes_ref[:, :T] + 3
        a = jnp.where(a >= PRIME, a - PRIME, a)
        a = jnp.where(live, a, 0)
        at_ref[...] = a.astype(F32).T
        b = codes_ref[:, T:] + 1
        b_ref[...] = jnp.where(b >= PRIME, b - PRIME, b).astype(F32)

    def mask_group(g):
        at = at_ref[...]
        for u in range(8):
            s = g * 8 + u
            prod = at[:, u : u + 1] * b_ref[s : s + 1, :]
            near_q = (prod * (1.0 / PRIME) + ROUND) - ROUND
            left = prod - near_q * PRIME
            hit = (left >= 3.0) & (left < 67.0)
            masks_ref[s * T : (s + 1) * T, :] = jnp.where(hit, 1.0, 0.0).astype(BF16)
        at_ref[...] = pltpu.roll(at, T - 8, 1)

    plan.filler(codes_ready, 0.3)
    for g in range(SLOTS // 8):
        plan.filler(functools.partial(mask_group, g), 0.35)
    plan.filler(tables, 0.8)
    plan.run()
    return [plan]


UNROLL = 8


def tile_at(t):
    return pl.ds(t * T, T)


def product_part(forward, tiles, tab_ref, masks_ref, src_ref, out_ref, pre_ref):
    base = 0 if forward else 5

    def step(g, acc):
        for u in range(UNROLL):
            j = g * UNROLL + u
            mask = masks_ref[tile_at(tab_ref[base, j]), :]
            src = src_ref[tile_at(tab_ref[base + 1, j]), :]
            new = jnp.dot(mask, src, preferred_element_type=F32) if forward else jnp.dot(src, mask, preferred_element_type=F32)
            acc = acc * tab_ref[base + 2, j].astype(F32) + new
            pre_ref[tile_rows(j), :] = acc
        return acc

    lax.fori_loop(0, SLOTS // UNROLL, step, jnp.zeros((T, T), F32))
    for t in range(tiles):
        v = pre_ref[tile_at(tab_ref[base + 3, t]), :]
        out_ref[t * T : (t + 1) * T, :] = (v * tab_ref[base + 4, t].astype(F32)).astype(BF16)


W1 = T // 2
WZ = W1 // NZ


def dense_part(
    me, root, rp_ref, weight_ref, bias_ref, cot_ref, hid_ref, gt_ref, gsum_ref,
    acc_ref, cs_ref, zs_ref, gl_ref, g1_ref, gz_ref, g2_ref,
):
    core, mz = me.core, me.mz
    plan = Plan()
    offsets = around(NZ)
    for i, o in enumerate(offsets):
        plan.message(
            ("c", o), ("c", 1), 65536,
            me.copier(
                functools.partial(lambda p: rp_ref.at[rows_of(p, 0, PIECE), :], me.z_piece(o, 1 - core)),
                functools.partial(lambda i: cs_ref.at[pl.ds(i * PIECE, PIECE), :], i),
                me.other,
            ),
        )
        plan.action([], None, [("c", o)], 0.05)
    legs = {}
    base = 0
    for d in (1, -1):
        for k in range(NZ // 2, 0, -1):
            first, size = (0, PIECE) if k < NZ // 2 else half(0, PIECE, d)
            piece = me.z_piece(d * k, core)
            legs[d, k] = (base, first, size, piece)
            plan.message(
                ("z", d, k), ("z", d), size * 256,
                me.copier(
                    functools.partial(lambda p, f, s: acc_ref.at[rows_of(p, f, s), :], piece, first, size),
                    functools.partial(lambda b, s: zs_ref.at[pl.ds(b, s), :], base, size),
                    me.at_z(d),
                ),
            )
            base += size

    def z_add(d, k):
        o = NZ // 2 if k == NZ // 2 else d * k
        _, first, size, piece = legs[d, k]
        given = [(cs_ref, offsets.index(o) * PIECE + first, first, size)]
        if k < NZ // 2:
            b, f, n, _ = legs[d, k + 1]
            given.append((zs_ref, b, f, n))
        combine(acc_ref, rp_ref, piece, first, size, given)

    for k in range(NZ // 2, 0, -1):
        for d in (1, -1):
            deps = [("c", NZ // 2 if k == NZ // 2 else d * k)]
            if k < NZ // 2:
                deps.append(("z", d, k + 1))
            plan.action(deps, functools.partial(z_add, d, k), [("z", d, k)], 0.08)
    plan.run()

    i0 = offsets.index(0)
    agg_sum = rp_ref[rows_of(me.col, 0, PIECE), :].astype(F32) + cs_ref[i0 * PIECE : (i0 + 1) * PIECE, :].astype(F32)
    for d in (1, -1):
        b = legs[d, 1][0]
        agg_sum = agg_sum + zs_ref[b : b + PIECE, :].astype(F32)
    spread = jnp.concatenate([jnp.broadcast_to(root[h : h + 1, :], (T, T)).T for h in range(2)], axis=0)
    aggregate = (spread * agg_sum).astype(BF16)
    weight = weight_ref[...]
    preact = jnp.dot(aggregate, weight, preferred_element_type=F32) + bias_ref[...]
    below = jnp.exp(jnp.minimum(preact, 0.0))
    hid_ref[...] = jnp.where(preact > 0, preact, below - 1.0).astype(BF16)
    grad_pre = cot_ref[...].astype(F32) * jnp.where(preact > 0, 1.0, below)
    grad_pre_b = grad_pre.astype(BF16)
    grad_agg_t = lax.dot_general(weight, grad_pre_b, (((1,), (1,)), ((), ())), preferred_element_type=F32)
    for h in range(2):
        gt_ref[rows_of(me.col, h * T, T), :] = (grad_agg_t[:, h * T : (h + 1) * T] * root[h : h + 1, :]).astype(BF16)

    plan2 = Plan()
    for d in (1, -1):
        for k in range(1, NZ // 2 + 1):
            first, size = (0, PIECE) if k < NZ // 2 else half(0, PIECE, d)
            piece = me.z_piece(-d * (k - 1), core)
            where = functools.partial(lambda p, f, s: gt_ref.at[rows_of(p, f, s), :], piece, first, size)
            plan2.message(("Z", d, k), ("z", d), size * 256, me.copier(where, where, me.at_z(d)))
    for o in offsets:
        where = functools.partial(lambda p: gt_ref.at[rows_of(p, 0, PIECE), :], me.z_piece(o, core))
        plan2.message(("C", o), ("c", 1), 65536, me.copier(where, where, me.other))
    plan2.action([], None, [("Z", 1, 1), ("Z", -1, 1), ("C", 0)])
    for d in (1, -1):
        for k in range(2, NZ // 2 + 1):
            plan2.action([("Z", d, k - 1)], None, [("Z", d, k)])
    for k in range(1, NZ // 2 + 1):
        if k == NZ // 2:
            plan2.action([("Z", 1, k), ("Z", -1, k)], None, [("C", k)])
        else:
            for d in (1, -1):
                plan2.action([("Z", d, k)], None, [("C", -d * k)])

    scale = 1.0 / math.sqrt(PIECE * NX * NY * NZ * 2)

    def grads():
        agg_t = aggregate.astype(F32).T.astype(BF16)
        gw = jnp.dot(agg_t, grad_pre_b, preferred_element_type=F32) * scale
        gb = jnp.sum(grad_pre, axis=0, keepdims=True) * scale
        gb8 = jnp.where(lax.broadcasted_iota(I32, (8, T), 0) == 0, gb, 0.0)
        for k in range(2):
            gl_ref[k * 72 : k * 72 + W1, :] = gw[k * W1 : (k + 1) * W1, :]
            gl_ref[k * 72 + W1 : (k + 1) * 72, :] = gb8

    plan2.message(
        ("G", 1), ("c", 1), 72 * 512,
        me.copier(lambda: gl_ref.at[slots_of(1 - core, 72), :], lambda: g1_ref.at[:, :], me.other),
    )
    plan2.action([], grads, [("G", 1)], 0.5)
    g2 = []
    for o in range(1, NZ):
        g2.append(("G2", o))
        plan2.message(
            ("G2", o), ("gz", o), 16 * 512,
            me.copier(
                functools.partial(lambda o: gz_ref.at[slots_of(lax.rem(mz + o, NZ), 16), :], o),
                lambda: g2_ref.at[slots_of(mz, 16), :],
                me.at_z(o),
            ),
        )

    def after_chip():
        total = gl_ref[slots_of(core, 72), :] + g1_ref[...]
        for z in range(NZ):
            gz_ref[z * 16 : z * 16 + 8, :] = total[z * WZ : (z + 1) * WZ, :]
            gz_ref[z * 16 + 8 : z * 16 + 16, :] = total[W1 : W1 + 8, :]
        g2_ref[slots_of(mz, 16), :] = gz_ref[slots_of(mz, 16), :]

    plan2.action([("G", 1)], after_chip, g2, 0.2)

    def after_z():
        gsum_ref[...] = total_of(g2_ref, NZ)

    plan2.action(g2, after_z, (), 0.1)
    plan2.run()
    return [plan, plan2]


def total_of(ref, n):
    v = ref[0:16, :]
    for i in range(1, n):
        v = v + ref[i * 16 : (i + 1) * 16, :]
    return v


def scatter_part(me, root, cp_ref, gsum_ref, gf_ref, gw_ref, gb_ref, acc_ref, sum_ref, g3_ref, g3x_ref, g4_ref, yx_ref):
    core, mz, mx, my = me.core, me.mz, me.mx, me.my
    plan = Plan()
    slot_rows = [0]

    def leg(which, axis, o, d, k, src):
        n = NX if axis == "x" else NY
        first, size = part_rows(which, d, k == n // 2)
        piece = me.xy_piece(d * k, o) if axis == "x" else me.xy_piece(o, d * k)
        base = slot_rows[0]
        slot_rows[0] += size
        dev = me.at_xy(d, 0) if axis == "x" else me.at_xy(0, d)
        key = ("s", which, axis, o, d, k)
        plan.message(
            key, (axis, d), size * 256,
            me.copier(
                lambda: src.at[rows_of(piece, first, size), :], lambda: sum_ref.at[pl.ds(base, size), :], dev
            ),
        )
        return dict(key=key, base=base, first=first, size=size, piece=piece)

    def given(*legs):
        return [(sum_ref, e["base"], e["first"], e["size"]) for e in legs]

    def adder(leg, *others):
        return lambda: combine(acc_ref, cp_ref, leg["piece"], leg["first"], leg["size"], given(*others))

    finals = {}
    late = []
    for which, one, two in (("A", "y", "x"), ("B", "x", "y")):
        n1 = NX if one == "x" else NY
        n2 = NX if two == "x" else NY
        done = {}
        for o in around(n2):
            ends = []
            for d in (1, -1):
                prev = None
                for k in range(n1 // 2, 0, -1):
                    now = leg(which, one, o, d, k, cp_ref if prev is None else acc_ref)
                    if prev is None:
                        plan.action([], None, [now["key"]])
                    else:
                        late.append(([prev["key"]], adder(now, prev), [now["key"]], 0.05))
                    prev = now
                ends.append(prev)
            done[o] = ends
        legs = {}
        for d in (1, -1):
            for k in range(n2 // 2, 0, -1):
                now = legs[d, k] = leg(which, two, 0, d, k, acc_ref)
                more = done[n2 // 2 if k == n2 // 2 else d * k] + ([legs[d, k + 1]] if k < n2 // 2 else [])
                late.append(([e["key"] for e in more], adder(now, *more), [now["key"]], 0.08))
        finals[which] = done[0] + [legs[1, 1], legs[-1, 1]]
    for deps, fn, sends, cost in late:
        plan.action(deps, fn, sends, cost)

    def ride(tag, n, dev, where, size):
        keys = []
        for o in range(1, n):
            keys.append((tag, o))
            plan.message((tag, o), (tag, o), size * 512, me.copier(where, where, dev(o)))
        return keys

    g3x = ride("G3x", NX, lambda o: me.at_xy(o, 0), lambda: g3x_ref.at[slots_of(mx, 16), :], 16)

    def start_x():
        g3x_ref[slots_of(mx, 16), :] = gsum_ref[...]

    plan.action([], start_x, g3x, 0.02)
    g3y = ride("G3y", NY, lambda o: me.at_xy(0, o), lambda: g3_ref.at[slots_of(my, 16), :], 16)

    def after_x():
        g3_ref[slots_of(my, 16), :] = total_of(g3x_ref, NX)

    plan.action(g3x, after_x, g3y, 0.05)
    own_w = lambda: pl.ds(pl.multiple_of(core * W1 + mz * WZ, 8), WZ)
    g4 = ride("G4", NZ, me.at_z, lambda: g4_ref.at[own_w(), :], WZ)

    def after_y():
        v = total_of(g3_ref, NY)
        gb_ref[...] = v[8:9, :]
        g4_ref[own_w(), :] = v[0:8, :]

    plan.action(g3y, after_y, g4, 0.05)
    half_w = lambda: g4_ref.at[slots_of(core, W1), :]
    plan.message(("G5", 0), ("c", 1), W1 * 512, me.copier(half_w, half_w, me.other))
    plan.action(g4, None, [("G5", 0)])

    def give_weight():
        gw_ref[...] = g4_ref[...]

    plan.action([("G5", 0)], give_weight, (), 0.05)
    plan.run()

    for which in ("A", "B"):
        first, size = PARTS[which]
        v = cp_ref[rows_of(me.row, first, size), :].astype(F32)
        for e in finals[which]:
            v = v + sum_ref[pl.ds(e["base"], e["size"]), :].astype(F32)
        yx_ref[first : first + size, :] = v
    for h in range(2):
        v = yx_ref[h * T : (h + 1) * T, :] * root[h : h + 1, :]
        gf_ref[h * T : (h + 1) * T, :] = v.T.astype(BF16)
    return [plan]


COPIES = 76 + 40 + 94
ROW_NODES = PIECE * NZ * 2
COL_NODES = PIECE * NX * NY


def body(
    feat_ref, deg_ref, weight_ref, bias_ref, cot_ref, rows_ref, cols_ref, count_ref, codes_ref,
    hid_ref, gf_ref, gw_ref, gb_ref,
    xg_ref, masks_ref, tab_ref, at_ref, b_ref, pre_ref, rp_ref, racc_ref, cs_ref, zs_ref, gt_ref, cp_ref, cacc_ref,
    sum_ref, gsum_ref, gl_ref, g1_ref, gz_ref, g2_ref, g3_ref, g3x_ref, g4_ref, yx_ref,
    tab_s, tab_sem, send_sem, recv_sem,
):
    me = Place(send_sem, recv_sem)
    met = me.enter([
        me.at_xy(1, 0), me.at_xy(-1, 0), me.at_xy(0, 1), me.at_xy(0, -1), me.at_z(1), me.at_z(-1), me.other,
    ])
    root = lax.rsqrt(deg_ref[...].astype(F32))
    tab_ref[...] = jnp.zeros_like(tab_ref)
    plans = gather_part(
        me, root, met, feat_ref, rows_ref, cols_ref, count_ref, codes_ref, xg_ref, masks_ref, tab_ref, at_ref, b_ref
    )
    moved = pltpu.make_async_copy(tab_ref, tab_s, tab_sem)
    moved.start()
    moved.wait()
    product_part(True, ROW_NODES // T, tab_s, masks_ref, xg_ref, rp_ref, pre_ref)
    plans += dense_part(
        me, root, rp_ref, weight_ref, bias_ref, cot_ref, hid_ref, gt_ref, gsum_ref,
        racc_ref, cs_ref, zs_ref, gl_ref, g1_ref, gz_ref, g2_ref,
    )
    product_part(False, COL_NODES // T, tab_s, masks_ref, gt_ref, cp_ref, pre_ref)
    plans += scatter_part(
        me, root, cp_ref, gsum_ref, gf_ref, gw_ref, gb_ref, cacc_ref, sum_ref, g3_ref, g3x_ref, g4_ref, yx_ref
    )
    for plan in plans:
        plan.drain()


def local(features, degree, weight, bias, cotangent, tile_rows, tile_cols, tile_count, tile_codes):
    vmem = pl.BlockSpec(memory_space=pltpu.VMEM)
    smem = pl.BlockSpec(memory_space=pltpu.SMEM)
    hidden, grad_features, grad_weight, grad_bias = pl.pallas_call(
        body,
        out_shape=(
            jax.ShapeDtypeStruct((PIECE, T), BF16),
            jax.ShapeDtypeStruct((PIECE, T), BF16),
            jax.ShapeDtypeStruct((T, T), F32),
            jax.ShapeDtypeStruct((1, T), F32),
        ),
        in_specs=[vmem] * 7 + [smem, vmem],
        out_specs=(vmem,) * 4,
        scratch_shapes=[
            pltpu.VMEM((COL_NODES, T), BF16),
            pltpu.VMEM((SLOTS * T, T), BF16),
            pltpu.VMEM((16, T), I32),
            pltpu.VMEM((T, SLOTS), F32),
            pltpu.VMEM((SLOTS, T), F32),
            pltpu.VMEM((SLOTS * T, T), F32),
            pltpu.VMEM((ROW_NODES, T), BF16),
            pltpu.VMEM((ROW_NODES, T), BF16),
            pltpu.VMEM((PIECE * NZ, T), BF16),
            pltpu.VMEM((PIECE * (NZ - 1), T), BF16),
            pltpu.VMEM((ROW_NODES, T), BF16),
            pltpu.VMEM((COL_NODES, T), BF16),
            pltpu.VMEM((COL_NODES, T), BF16),
            pltpu.VMEM((COL_NODES - PIECE, T), BF16),
            pltpu.VMEM((16, T), F32),
            pltpu.VMEM((144, T), F32),
            pltpu.VMEM((72, T), F32),
            pltpu.VMEM((16 * NZ, T), F32),
            pltpu.VMEM((16 * NZ, T), F32),
            pltpu.VMEM((16 * NY, T), F32),
            pltpu.VMEM((16 * NX, T), F32),
            pltpu.VMEM((T, T), F32),
            pltpu.VMEM((PIECE, T), F32),
            pltpu.SMEM((16, T), I32),
            pltpu.SemaphoreType.DMA,
            pltpu.SemaphoreType.DMA((COPIES,)),
            pltpu.SemaphoreType.DMA((COPIES,)),
        ],
        compiler_params=pltpu.CompilerParams(collective_id=0, has_side_effects=True),
        name="layer",
    )(
        features,
        degree.reshape(2, T),
        weight,
        bias.reshape(1, T),
        cotangent,
        tile_rows.reshape(1, SLOTS),
        tile_cols.reshape(1, SLOTS),
        tile_count.reshape(1, 1),
        tile_codes.reshape(SLOTS, 2 * T),
    )
    return hidden, grad_features, grad_weight, grad_bias.reshape(T)


def solution(mesh):
    placed = (
        P(("row", "col"), None),
        P(("row", "col")),
        P(),
        P(),
        P(("row", "col"), None),
        P("row", "col", None),
        P("row", "col", None),
        P("row", "col", None),
        P("row", "col", None, None),
    )
    return jax.shard_map(
        local,
        mesh=mesh,
        in_specs=placed,
        out_specs=(P(("row", "col"), None), P(("row", "col"), None), P(), P()),
        check_vma=False,
    )
```

```python
import functools
import math

import jax
import jax.numpy as jnp
from jax import lax
from jax.experimental import pallas as pl
from jax.experimental.pallas import tpu as pltpu
from jax.sharding import PartitionSpec as P

MESH = pl.DeviceIdType.MESH
F32 = jnp.float32
BF16 = jnp.bfloat16
I32 = jnp.int32

NX, NY, NZ = 4, 8, 8
PIECE = 256
T = 128
SLOTS = 128
PRIME = 4093
ROUND = 12582912.0
CUT = 96

WIRE = 46e3
CORE_WIRE = 250e3
HOP = 2.5
HOP_MORE = 0.5
CORE_HOP = 0.95


class Plan:
    def __init__(self):
        self.copies = {}
        self.actions = []
        self.fillers = []

    def message(self, key, link, nbytes, make):
        self.copies[key] = [link, nbytes, make, None]

    def action(self, deps, fn, sends=(), cost=0.03):
        self.actions.append((tuple(deps), fn, tuple(sends), cost))

    def filler(self, fn, cost):
        self.fillers.append((fn, cost))

    def run(self, leave=()):
        now = 0.0
        free = {}
        arrival = {}
        todo = list(self.actions)
        fill = list(self.fillers)
        waited = set()
        while todo:
            best, best_at = None, None
            for item in todo:
                if all(d in arrival for d in item[0]):
                    at = max([now] + [arrival[d] for d in item[0]])
                    if best is None or at < best_at - 1e-9:
                        best, best_at = item, at
            if fill and best_at > now + 0.1:
                fn, cost = fill.pop(0)
                fn()
                now += cost
                continue
            deps, fn, sends, cost = best
            todo.remove(best)
            for d in sorted(deps, key=lambda d: arrival[d]):
                if d not in waited:
                    waited.add(d)
                    self.copies[d][3].wait_recv()
            now = best_at
            if fn is not None:
                fn()
                now += cost
            for key in sends:
                link, nbytes, make, _ = self.copies[key]
                copy = make()
                self.copies[key][3] = copy
                copy.start()
                hops = link[2] if len(link) > 2 else 1
                wire, hop = (CORE_WIRE, CORE_HOP) if link[0] == "c" else (WIRE, HOP + HOP_MORE * (hops - 1))
                link = link[:2]
                free[link] = max(free.get(link, 0.0), now) + nbytes * hops / wire
                arrival[key] = free[link] + hop
        for fn, cost in fill:
            fn()
        for key, item in self.copies.items():
            if key not in waited and key not in leave:
                item[3].wait_recv()

    def drain(self):
        for item in self.copies.values():
            item[3].wait_send()


class Place:
    def __init__(self, send_sem, recv_sem):
        self.row = row = lax.axis_index("row")
        self.col = col = lax.axis_index("col")
        self.mx, self.my = row // NY, row % NY
        self.mz, self.core = col // 2, col % 2
        self.other = (row, self.mz * 2 + (1 - self.core))
        self.send_sem, self.recv_sem = send_sem, recv_sem
        self.used = 0

    def xy_piece(self, x, y):
        return lax.rem(self.mx + x + NX, NX) * NY + lax.rem(self.my + y + NY, NY)

    def z_piece(self, z, k):
        return lax.rem(self.mz + z + NZ, NZ) * 2 + k

    def at_xy(self, x, y):
        return (self.xy_piece(x, y), self.col)

    def at_z(self, z):
        return (self.row, self.z_piece(z, self.core))

    def copier(self, src, dst, dev):
        i = self.used
        self.used += 1

        def make():
            return pltpu.make_async_remote_copy(
                src_ref=src(), dst_ref=dst(), send_sem=self.send_sem.at[i], recv_sem=self.recv_sem.at[i],
                device_id=dev, device_id_type=MESH,
            )

        return make

    def enter(self, peers):
        barrier = pltpu.get_barrier_semaphore()
        for dev in peers:
            pl.semaphore_signal(barrier, inc=1, device_id=dev, device_id_type=MESH)

        def met():
            pl.semaphore_wait(barrier, len(peers))

        return met


def rows_of(start, first, size):
    return pl.ds(pl.multiple_of(start * PIECE + first, 16), size)


def tile_rows(t):
    return pl.ds(pl.multiple_of(t * T, T), T)


def slots_of(i, n):
    return pl.ds(pl.multiple_of(i * n, 8), n)


PARTS = {"A": (0, CUT), "B": (CUT, PIECE - CUT)}


def half(first, size, d):
    return (first, size // 2) if d > 0 else (first + size // 2, size // 2)


def part_rows(which, d, last):
    first, size = PARTS[which]
    return half(first, size, d) if last else (first, size)


def combine(dst, src, piece, first, size, given):
    whole = all(n >= size for _, _, _, n in given)
    blocks = [(first, size)] if whole else [half(first, size, 1), half(first, size, -1)]
    for f, n in blocks:
        v = src[rows_of(piece, f, n), :].astype(F32)
        for ref, base, gf, gn in given:
            if gf <= f and f + n <= gf + gn:
                v = v + ref[pl.ds(base + f - gf, n), :].astype(F32)
        dst[rows_of(piece, f, n), :] = v.astype(BF16)


CHAIN4 = ((0, 1), (1, 1))
DIRECT4 = ((0, 1), (0, 2))
CHAIN8 = ((0, 1), (1, 1), (2, 1), (3, 1))
TWO8 = ((0, 2), (0, 1), (2, 2), (2, 1))
STEPS = {("A", "x"): DIRECT4, ("A", "y"): TWO8, ("B", "y"): TWO8, ("B", "x"): CHAIN4}
STEPS_Z = TWO8


def around(n):
    out = [n // 2]
    for k in range(n // 2 - 1, 0, -1):
        out += [k, -k]
    return out + [0]


def gather_part(me, root, met, feat_ref, rows_ref, cols_ref, count_ref, codes_ref, xg_ref, masks_ref, tab_ref, at_ref, b_ref):
    for h in range(2):
        spread = jnp.broadcast_to(root[h : h + 1, :], (T, T)).T
        xg_ref[rows_of(me.row, h * T, T), :] = (spread * feat_ref[h * T : (h + 1) * T, :].astype(F32)).astype(BF16)
    met()
    plan = Plan()

    def leg(which, axis, o, d, b, h):
        n = NX if axis == "x" else NY
        first, size = part_rows(which, d, b + h == n // 2)
        piece = me.xy_piece(-d * b, o) if axis == "x" else me.xy_piece(o, -d * b)
        where = lambda: xg_ref.at[rows_of(piece, first, size), :]
        dev = me.at_xy(d * h, 0) if axis == "x" else me.at_xy(0, d * h)
        key = (which, axis, o, d, b + h)
        plan.message(key, (axis, d, h), size * 256, me.copier(where, where, dev))
        return key

    for which, one in (("A", "x"), ("B", "y")):
        for b, h in STEPS[which, one]:
            for d in (1, -1):
                need = [(which, one, 0, d, b)] if b else []
                plan.action(need, None, [leg(which, one, 0, d, b, h)])
    for which, one, two in (("A", "x", "y"), ("B", "y", "x")):
        n1 = NX if one == "x" else NY
        for o in around(n1)[::-1]:
            if o == 0:
                have = []
            elif o == n1 // 2:
                have = [(which, one, 0, 1, o), (which, one, 0, -1, o)]
            else:
                have = [(which, one, 0, -1 if o > 0 else 1, abs(o))]
            for b, h in STEPS[which, two]:
                for d in (1, -1):
                    need = [(which, two, o, d, b)] if b else have
                    plan.action(need, None, [leg(which, two, o, d, b, h)])

    def tables():
        lane = lax.broadcasted_iota(I32, (T, T), 1)
        sub = lax.broadcasted_iota(I32, (T, T), 0)
        out = []
        spread = [jnp.broadcast_to(v, (T, T)) for v in (rows_ref[...], cols_ref[...])]
        stood = [v.T for v in spread]
        for mine in (0, 1):
            key_l = spread[mine] * SLOTS + lane
            key_s = stood[mine] * SLOTS + sub
            rank = jnp.sum((key_s < key_l).astype(I32), axis=0, keepdims=True)
            hot = jnp.broadcast_to(rank, (T, T)).T == lane
            pick = lambda v: jnp.sum(jnp.where(hot, v, 0), axis=0, keepdims=True)
            order = pick(sub)
            target = pick(stood[mine])
            source = pick(stood[1 - mine])
            same = (target == pltpu.roll(target, 1, 1)) & (lane[:1] > 0)
            last = jnp.sum((stood[mine] <= lane).astype(I32), axis=0, keepdims=True) - 1
            has = jnp.sum((stood[mine] == lane).astype(I32), axis=0, keepdims=True)
            out += [order, source, same.astype(I32), jnp.maximum(last, 0), (has > 0).astype(I32)]
        for i, v in enumerate(out):
            tab_ref[i : i + 1, :] = v

    def codes_ready():
        live = lax.broadcasted_iota(I32, (SLOTS, T), 0) < count_ref[0, 0]
        a = codes_ref[:, :T] + 3
        a = jnp.where(a >= PRIME, a - PRIME, a)
        a = jnp.where(live, a, 0)
        at_ref[...] = a.astype(F32).T
        b = codes_ref[:, T:] + 1
        b_ref[...] = jnp.where(b >= PRIME, b - PRIME, b).astype(F32)

    def mask_group(g):
        at = at_ref[...]
        for u in range(8):
            s = g * 8 + u
            prod = at[:, u : u + 1] * b_ref[s : s + 1, :]
            near_q = (prod * (1.0 / PRIME) + ROUND) - ROUND
            left = prod - near_q * PRIME
            hit = (left >= 3.0) & (left < 67.0)
            masks_ref[s * T : (s + 1) * T, :] = jnp.where(hit, 1.0, 0.0).astype(BF16)
        at_ref[...] = pltpu.roll(at, T - 8, 1)

    plan.filler(codes_ready, 0.3)
    for g in range(SLOTS // 8):
        plan.filler(functools.partial(mask_group, g), 0.35)
    plan.filler(tables, 0.8)
    plan.run()
    return [plan]


UNROLL = 8


def tile_at(t):
    return pl.ds(t * T, T)


def product_part(forward, tiles, tab_ref, masks_ref, src_ref, out_ref, pre_ref):
    base = 0 if forward else 5

    def step(g, acc):
        for u in range(UNROLL):
            j = g * UNROLL + u
            mask = masks_ref[tile_at(tab_ref[base, j]), :]
            src = src_ref[tile_at(tab_ref[base + 1, j]), :]
            new = jnp.dot(mask, src, preferred_element_type=F32) if forward else jnp.dot(src, mask, preferred_element_type=F32)
            acc = acc * tab_ref[base + 2, j].astype(F32) + new
            pre_ref[tile_rows(j), :] = acc
        return acc

    lax.fori_loop(0, SLOTS // UNROLL, step, jnp.zeros((T, T), F32))
    for t in range(tiles):
        v = pre_ref[tile_at(tab_ref[base + 3, t]), :]
        out_ref[t * T : (t + 1) * T, :] = (v * tab_ref[base + 4, t].astype(F32)).astype(BF16)


W1 = T // 2
WZ = W1 // NZ


def dense_part(
    me, root, rp_ref, weight_ref, bias_ref, cot_ref, hid_ref, gt_ref, gsum_ref,
    acc_ref, cs_ref, zs_ref, gl_ref, g1_ref, gz_ref, g2_ref,
):
    core, mz = me.core, me.mz
    plan = Plan()
    offsets = around(NZ)
    for i, o in enumerate(offsets):
        plan.message(
            ("c", o), ("c", 1), 65536,
            me.copier(
                functools.partial(lambda p: rp_ref.at[rows_of(p, 0, PIECE), :], me.z_piece(o, 1 - core)),
                functools.partial(lambda i: cs_ref.at[pl.ds(i * PIECE, PIECE), :], i),
                me.other,
            ),
        )
        plan.action([], None, [("c", o)], 0.05)
    legs = {}
    base = 0
    for d in (1, -1):
        for b, h in STEPS_Z:
            first, size = half(0, PIECE, d) if b + h == NZ // 2 else (0, PIECE)
            piece = me.z_piece(d * (b + h), core)
            legs[d, b, h] = (base, first, size, piece)
            plan.message(
                ("z", d, b, h), ("z", d, h), size * 256,
                me.copier(
                    functools.partial(lambda p, f, s: acc_ref.at[rows_of(p, f, s), :], piece, first, size),
                    functools.partial(lambda b, s: zs_ref.at[pl.ds(b, s), :], base, size),
                    me.at_z(d * h),
                ),
            )
            base += size

    def z_add(d, b, h, before):
        o = NZ // 2 if b + h == NZ // 2 else d * (b + h)
        _, first, size, piece = legs[d, b, h]
        given = [(cs_ref, offsets.index(o) * PIECE, 0, PIECE)] + [(zs_ref,) + legs[k][:3] for k in before]
        combine(acc_ref, rp_ref, piece, first, size, given)

    for b, h in sorted(STEPS_Z, key=lambda s: (-s[0], -s[1])):
        for d in (1, -1):
            before = [(d, b2, h2) for b2, h2 in STEPS_Z if b2 == b + h]
            deps = [("c", NZ // 2 if b + h == NZ // 2 else d * (b + h))] + [("z",) + k for k in before]
            plan.action(deps, functools.partial(z_add, d, b, h, before), [("z", d, b, h)], 0.1)
    plan.run()

    i0 = offsets.index(0)
    agg_sum = rp_ref[rows_of(me.col, 0, PIECE), :].astype(F32) + cs_ref[i0 * PIECE : (i0 + 1) * PIECE, :].astype(F32)
    for (d, b, h), (base, _, size, _) in legs.items():
        if b == 0:
            agg_sum = agg_sum + zs_ref[base : base + PIECE, :].astype(F32)
    spread = jnp.concatenate([jnp.broadcast_to(root[h : h + 1, :], (T, T)).T for h in range(2)], axis=0)
    aggregate = (spread * agg_sum).astype(BF16)
    weight = weight_ref[...]
    preact = jnp.dot(aggregate, weight, preferred_element_type=F32) + bias_ref[...]
    below = jnp.exp(jnp.minimum(preact, 0.0))
    hid_ref[...] = jnp.where(preact > 0, preact, below - 1.0).astype(BF16)
    grad_pre = cot_ref[...].astype(F32) * jnp.where(preact > 0, 1.0, below)
    grad_pre_b = grad_pre.astype(BF16)
    grad_agg_t = lax.dot_general(weight, grad_pre_b, (((1,), (1,)), ((), ())), preferred_element_type=F32)
    for h in range(2):
        gt_ref[rows_of(me.col, h * T, T), :] = (grad_agg_t[:, h * T : (h + 1) * T] * root[h : h + 1, :]).astype(BF16)

    plan2 = Plan()
    for b, h in STEPS_Z:
        for d in (1, -1):
            first, size = half(0, PIECE, d) if b + h == NZ // 2 else (0, PIECE)
            piece = me.z_piece(-d * b, core)
            where = functools.partial(lambda p, f, s: gt_ref.at[rows_of(p, f, s), :], piece, first, size)
            plan2.message(("Z", d, b + h), ("z", d, h), size * 256, me.copier(where, where, me.at_z(d * h)))
            plan2.action([("Z", d, b)] if b else [], None, [("Z", d, b + h)])
    for o in offsets:
        where = functools.partial(lambda p: gt_ref.at[rows_of(p, 0, PIECE), :], me.z_piece(o, core))
        plan2.message(("C", o), ("c", 1), 65536, me.copier(where, where, me.other))
    plan2.action([], None, [("C", 0)])
    for k in range(1, NZ // 2 + 1):
        if k == NZ // 2:
            plan2.action([("Z", 1, k), ("Z", -1, k)], None, [("C", k)])
        else:
            for d in (1, -1):
                plan2.action([("Z", d, k)], None, [("C", -d * k)])

    scale = 1.0 / math.sqrt(PIECE * NX * NY * NZ * 2)

    def grads():
        agg_t = aggregate.astype(F32).T.astype(BF16)
        gw = jnp.dot(agg_t, grad_pre_b, preferred_element_type=F32) * scale
        gb = jnp.sum(grad_pre, axis=0, keepdims=True) * scale
        gb8 = jnp.where(lax.broadcasted_iota(I32, (8, T), 0) == 0, gb, 0.0)
        for k in range(2):
            gl_ref[k * 72 : k * 72 + W1, :] = gw[k * W1 : (k + 1) * W1, :]
            gl_ref[k * 72 + W1 : (k + 1) * 72, :] = gb8

    plan2.message(
        ("G", 1), ("c", 1), 72 * 512,
        me.copier(lambda: gl_ref.at[slots_of(1 - core, 72), :], lambda: g1_ref.at[:, :], me.other),
    )
    plan2.action([], grads, [("G", 1)], 0.5)
    g2 = []
    for o in range(1, NZ):
        g2.append(("G2", o))
        plan2.message(
            ("G2", o), ("gz", o), 16 * 512,
            me.copier(
                functools.partial(lambda o: gz_ref.at[slots_of(lax.rem(mz + o, NZ), 16), :], o),
                lambda: g2_ref.at[slots_of(mz, 16), :],
                me.at_z(o),
            ),
        )

    def after_chip():
        total = gl_ref[slots_of(core, 72), :] + g1_ref[...]
        for z in range(NZ):
            gz_ref[z * 16 : z * 16 + 8, :] = total[z * WZ : (z + 1) * WZ, :]
            gz_ref[z * 16 + 8 : z * 16 + 16, :] = total[W1 : W1 + 8, :]
        g2_ref[slots_of(mz, 16), :] = gz_ref[slots_of(mz, 16), :]

    plan2.action([("G", 1)], after_chip, g2, 0.2)

    def after_z():
        gsum_ref[...] = total_of(g2_ref, NZ)

    plan2.action(g2, after_z, (), 0.1)
    plan2.run()
    return [plan, plan2]


def total_of(ref, n):
    v = ref[0:16, :]
    for i in range(1, n):
        v = v + ref[i * 16 : (i + 1) * 16, :]
    return v


def scatter_part(me, root, cp_ref, gsum_ref, gf_ref, gw_ref, gb_ref, acc_ref, sum_ref, g3_ref, g3x_ref, g4_ref, yx_ref):
    core, mz, mx, my = me.core, me.mz, me.mx, me.my
    plan = Plan()
    slot_rows = [0]

    def leg(which, axis, o, d, b, h, src):
        n = NX if axis == "x" else NY
        first, size = part_rows(which, d, b + h == n // 2)
        piece = me.xy_piece(d * (b + h), o) if axis == "x" else me.xy_piece(o, d * (b + h))
        base = slot_rows[0]
        slot_rows[0] += size
        dev = me.at_xy(d * h, 0) if axis == "x" else me.at_xy(0, d * h)
        key = ("s", which, axis, o, d, b, h)
        plan.message(
            key, (axis, d, h), size * 256,
            me.copier(
                lambda: src.at[rows_of(piece, first, size), :], lambda: sum_ref.at[pl.ds(base, size), :], dev
            ),
        )
        return dict(key=key, base=base, first=first, size=size, piece=piece)

    def given(*legs):
        return [(sum_ref, e["base"], e["first"], e["size"]) for e in legs]

    def adder(leg, *others):
        return lambda: combine(acc_ref, cp_ref, leg["piece"], leg["first"], leg["size"], given(*others))

    finals = {}
    late = []
    first_sends = []
    for which, one, two in (("A", "y", "x"), ("B", "x", "y")):
        n2 = NX if two == "x" else NY
        done = {}
        steps = sorted(STEPS[which, one], key=lambda s: (-s[0], -s[1]))
        for o in around(n2):
            done[o] = []
            for d in (1, -1):
                made = {}
                for b, h in steps:
                    prev = [made[k] for k in made if k[0] == b + h]
                    now = made[b, h] = leg(which, one, o, d, b, h, acc_ref if prev else cp_ref)
                    if prev:
                        late.append(([e["key"] for e in prev], adder(now, *prev), [now["key"]], 0.06))
                    else:
                        first_sends.append((b, now["key"]))
                    if b == 0:
                        done[o].append(now)
        finals[which] = list(done[0])
        for d in (1, -1):
            made = {}
            for b, h in sorted(STEPS[which, two], key=lambda s: (-s[0], -s[1])):
                prev = [made[k] for k in made if k[0] == b + h]
                now = made[b, h] = leg(which, two, 0, d, b, h, acc_ref)
                more = done[n2 // 2 if b + h == n2 // 2 else d * (b + h)] + prev
                late.append(([e["key"] for e in more], adder(now, *more), [now["key"]], 0.08))
                if b == 0:
                    finals[which].append(now)
    for _, key in sorted(first_sends, key=lambda e: -e[0]):
        plan.action([], None, [key])
    for deps, fn, sends, cost in late:
        plan.action(deps, fn, sends, cost)

    def ride(tag, n, dev, where, size):
        keys = []
        for o in range(1, n):
            keys.append((tag, o))
            plan.message((tag, o), (tag, o), size * 512, me.copier(where, where, dev(o)))
        return keys

    g3x = ride("G3x", NX, lambda o: me.at_xy(o, 0), lambda: g3x_ref.at[slots_of(mx, 16), :], 16)

    def start_x():
        g3x_ref[slots_of(mx, 16), :] = gsum_ref[...]

    plan.action([], start_x, g3x, 0.02)
    g3y = ride("G3y", NY, lambda o: me.at_xy(0, o), lambda: g3_ref.at[slots_of(my, 16), :], 16)

    def after_x():
        g3_ref[slots_of(my, 16), :] = total_of(g3x_ref, NX)

    plan.action(g3x, after_x, g3y, 0.05)
    own_w = lambda: pl.ds(pl.multiple_of(core * W1 + mz * WZ, 8), WZ)
    g4 = ride("G4", NZ, me.at_z, lambda: g4_ref.at[own_w(), :], WZ)

    def after_y():
        v = total_of(g3_ref, NY)
        gb_ref[...] = v[8:9, :]
        g4_ref[own_w(), :] = v[0:8, :]

    plan.action(g3y, after_y, g4, 0.05)
    half_w = lambda: g4_ref.at[slots_of(core, W1), :]
    plan.message(("G5", 0), ("c", 1), W1 * 512, me.copier(half_w, half_w, me.other))
    plan.action(g4, None, [("G5", 0)])

    def give_weight():
        gw_ref[...] = g4_ref[...]

    plan.action([("G5", 0)], give_weight, (), 0.05)
    plan.run()

    yx_ref[...] = cp_ref[rows_of(me.row, 0, PIECE), :].astype(F32)
    for e in finals["A"] + finals["B"]:
        at = slice(e["first"], e["first"] + e["size"])
        yx_ref[at, :] = yx_ref[at, :] + sum_ref[pl.ds(e["base"], e["size"]), :].astype(F32)
    for h in range(2):
        v = yx_ref[h * T : (h + 1) * T, :] * root[h : h + 1, :]
        gf_ref[h * T : (h + 1) * T, :] = v.T.astype(BF16)
    return [plan]


COPIES = 76 + 40 + 94
ROW_NODES = PIECE * NZ * 2
COL_NODES = PIECE * NX * NY


def body(
    feat_ref, deg_ref, weight_ref, bias_ref, cot_ref, rows_ref, cols_ref, count_ref, codes_ref,
    hid_ref, gf_ref, gw_ref, gb_ref,
    xg_ref, masks_ref, tab_ref, at_ref, b_ref, pre_ref, rp_ref, racc_ref, cs_ref, zs_ref, gt_ref, cp_ref, cacc_ref,
    sum_ref, gsum_ref, gl_ref, g1_ref, gz_ref, g2_ref, g3_ref, g3x_ref, g4_ref, yx_ref,
    tab_s, tab_sem, send_sem, recv_sem,
):
    me = Place(send_sem, recv_sem)
    met = me.enter(
        [me.at_xy(o, 0) for o in (1, 2, 3)]
        + [me.at_xy(0, o) for o in (1, 2, -2, -1)]
        + [me.at_z(o) for o in (1, 2, -2, -1)]
        + [me.other]
    )
    root = lax.rsqrt(deg_ref[...].astype(F32))
    tab_ref[...] = jnp.zeros_like(tab_ref)
    plans = gather_part(
        me, root, met, feat_ref, rows_ref, cols_ref, count_ref, codes_ref, xg_ref, masks_ref, tab_ref, at_ref, b_ref
    )
    moved = pltpu.make_async_copy(tab_ref, tab_s, tab_sem)
    moved.start()
    moved.wait()
    product_part(True, ROW_NODES // T, tab_s, masks_ref, xg_ref, rp_ref, pre_ref)
    plans += dense_part(
        me, root, rp_ref, weight_ref, bias_ref, cot_ref, hid_ref, gt_ref, gsum_ref,
        racc_ref, cs_ref, zs_ref, gl_ref, g1_ref, gz_ref, g2_ref,
    )
    product_part(False, COL_NODES // T, tab_s, masks_ref, gt_ref, cp_ref, pre_ref)
    plans += scatter_part(
        me, root, cp_ref, gsum_ref, gf_ref, gw_ref, gb_ref, cacc_ref, sum_ref, g3_ref, g3x_ref, g4_ref, yx_ref
    )
    for plan in plans:
        plan.drain()


def local(features, degree, weight, bias, cotangent, tile_rows, tile_cols, tile_count, tile_codes):
    vmem = pl.BlockSpec(memory_space=pltpu.VMEM)
    smem = pl.BlockSpec(memory_space=pltpu.SMEM)
    hidden, grad_features, grad_weight, grad_bias = pl.pallas_call(
        body,
        out_shape=(
            jax.ShapeDtypeStruct((PIECE, T), BF16),
            jax.ShapeDtypeStruct((PIECE, T), BF16),
            jax.ShapeDtypeStruct((T, T), F32),
            jax.ShapeDtypeStruct((1, T), F32),
        ),
        in_specs=[vmem] * 7 + [smem, vmem],
        out_specs=(vmem,) * 4,
        scratch_shapes=[
            pltpu.VMEM((COL_NODES, T), BF16),
            pltpu.VMEM((SLOTS * T, T), BF16),
            pltpu.VMEM((16, T), I32),
            pltpu.VMEM((T, SLOTS), F32),
            pltpu.VMEM((SLOTS, T), F32),
            pltpu.VMEM((SLOTS * T, T), F32),
            pltpu.VMEM((ROW_NODES, T), BF16),
            pltpu.VMEM((ROW_NODES, T), BF16),
            pltpu.VMEM((PIECE * NZ, T), BF16),
            pltpu.VMEM((PIECE * (NZ - 1), T), BF16),
            pltpu.VMEM((ROW_NODES, T), BF16),
            pltpu.VMEM((COL_NODES, T), BF16),
            pltpu.VMEM((COL_NODES, T), BF16),
            pltpu.VMEM((COL_NODES - PIECE, T), BF16),
            pltpu.VMEM((16, T), F32),
            pltpu.VMEM((144, T), F32),
            pltpu.VMEM((72, T), F32),
            pltpu.VMEM((16 * NZ, T), F32),
            pltpu.VMEM((16 * NZ, T), F32),
            pltpu.VMEM((16 * NY, T), F32),
            pltpu.VMEM((16 * NX, T), F32),
            pltpu.VMEM((T, T), F32),
            pltpu.VMEM((PIECE, T), F32),
            pltpu.SMEM((16, T), I32),
            pltpu.SemaphoreType.DMA,
            pltpu.SemaphoreType.DMA((COPIES,)),
            pltpu.SemaphoreType.DMA((COPIES,)),
        ],
        compiler_params=pltpu.CompilerParams(collective_id=0, has_side_effects=True),
        name="layer",
    )(
        features,
        degree.reshape(2, T),
        weight,
        bias.reshape(1, T),
        cotangent,
        tile_rows.reshape(1, SLOTS),
        tile_cols.reshape(1, SLOTS),
        tile_count.reshape(1, 1),
        tile_codes.reshape(SLOTS, 2 * T),
    )
    return hidden, grad_features, grad_weight, grad_bias.reshape(T)


def solution(mesh):
    placed = (
        P(("row", "col"), None),
        P(("row", "col")),
        P(),
        P(),
        P(("row", "col"), None),
        P("row", "col", None),
        P("row", "col", None),
        P("row", "col", None),
        P("row", "col", None, None),
    )
    return jax.shard_map(
        local,
        mesh=mesh,
        in_specs=placed,
        out_specs=(P(("row", "col"), None), P(("row", "col"), None), P(), P()),
        check_vma=False,
    )
```

```python
import functools
import math

import jax
import jax.numpy as jnp
from jax import lax
from jax.experimental import pallas as pl
from jax.experimental.pallas import tpu as pltpu
from jax.sharding import PartitionSpec as P

MESH = pl.DeviceIdType.MESH
F32 = jnp.float32
BF16 = jnp.bfloat16
I32 = jnp.int32

NX, NY, NZ = 4, 8, 8
PIECE = 256
T = 128
SLOTS = 128
PRIME = 4093
ROUND = 12582912.0
CUT = 128

WIRE = 46e3
CORE_WIRE = 250e3
HOP = 2.5
HOP_MORE = 0.5
CORE_HOP = 0.95


class Plan:
    def __init__(self):
        self.copies = {}
        self.actions = []
        self.fillers = []

    def message(self, key, link, nbytes, make):
        self.copies[key] = [link, nbytes, make, None]

    def action(self, deps, fn, sends=(), cost=0.03):
        self.actions.append((tuple(deps), fn, tuple(sends), cost))

    def filler(self, fn, cost):
        self.fillers.append((fn, cost))

    def run(self, leave=()):
        now = 0.0
        free = {}
        arrival = {}
        todo = list(self.actions)
        fill = list(self.fillers)
        waited = set()
        while todo:
            best, best_at = None, None
            for item in todo:
                if all(d in arrival for d in item[0]):
                    at = max([now] + [arrival[d] for d in item[0]])
                    if best is None or at < best_at - 1e-9:
                        best, best_at = item, at
            if fill and best_at > now + 0.1:
                fn, cost = fill.pop(0)
                fn()
                now += cost
                continue
            deps, fn, sends, cost = best
            todo.remove(best)
            for d in sorted(deps, key=lambda d: arrival[d]):
                if d not in waited:
                    waited.add(d)
                    self.copies[d][3].wait_recv()
            now = best_at
            if fn is not None:
                fn()
                now += cost
            for key in sends:
                link, nbytes, make, _ = self.copies[key]
                copy = make()
                self.copies[key][3] = copy
                copy.start()
                hops = link[2] if len(link) > 2 else 1
                wire, hop = (CORE_WIRE, CORE_HOP) if link[0] == "c" else (WIRE, HOP + HOP_MORE * (hops - 1))
                link = link[:2]
                free[link] = max(free.get(link, 0.0), now) + nbytes * hops / wire
                arrival[key] = free[link] + hop
        for fn, cost in fill:
            fn()
        for key, item in self.copies.items():
            if key not in waited and key not in leave:
                item[3].wait_recv()

    def drain(self):
        for item in self.copies.values():
            item[3].wait_send()


class Place:
    def __init__(self, send_sem, recv_sem):
        self.row = row = lax.axis_index("row")
        self.col = col = lax.axis_index("col")
        self.mx, self.my = row // NY, row % NY
        self.mz, self.core = col // 2, col % 2
        self.other = (row, self.mz * 2 + (1 - self.core))
        self.send_sem, self.recv_sem = send_sem, recv_sem
        self.used = 0

    def xy_piece(self, x, y):
        return lax.rem(self.mx + x + NX, NX) * NY + lax.rem(self.my + y + NY, NY)

    def z_piece(self, z, k):
        return lax.rem(self.mz + z + NZ, NZ) * 2 + k

    def at_xy(self, x, y):
        return (self.xy_piece(x, y), self.col)

    def at_z(self, z):
        return (self.row, self.z_piece(z, self.core))

    def copier(self, src, dst, dev):
        i = self.used
        self.used += 1

        def make():
            return pltpu.make_async_remote_copy(
                src_ref=src(), dst_ref=dst(), send_sem=self.send_sem.at[i], recv_sem=self.recv_sem.at[i],
                device_id=dev, device_id_type=MESH,
            )

        return make

    def enter(self, peers):
        barrier = pltpu.get_barrier_semaphore()
        for dev in peers:
            pl.semaphore_signal(barrier, inc=1, device_id=dev, device_id_type=MESH)

        def met():
            pl.semaphore_wait(barrier, len(peers))

        return met


def rows_of(start, first, size):
    return pl.ds(pl.multiple_of(start * PIECE + first, 16), size)


def tile_rows(t):
    return pl.ds(pl.multiple_of(t * T, T), T)


def slots_of(i, n):
    return pl.ds(pl.multiple_of(i * n, 8), n)


PARTS = {"A": (0, CUT), "B": (CUT, PIECE - CUT)}


def half(first, size, d):
    return (first, size // 2) if d > 0 else (first + size // 2, size // 2)


def part_rows(which, d, last):
    first, size = PARTS[which]
    return half(first, size, d) if last else (first, size)


def combine(dst, src, piece, first, size, given):
    whole = all(n >= size for _, _, _, n in given)
    blocks = [(first, size)] if whole else [half(first, size, 1), half(first, size, -1)]
    for f, n in blocks:
        v = src[rows_of(piece, f, n), :].astype(F32)
        for ref, base, gf, gn in given:
            if gf <= f and f + n <= gf + gn:
                v = v + ref[pl.ds(base + f - gf, n), :].astype(F32)
        dst[rows_of(piece, f, n), :] = v.astype(BF16)


CHAIN4 = ((0, 1), (1, 1))
DIRECT4 = ((0, 1), (0, 2))
CHAIN8 = ((0, 1), (1, 1), (2, 1), (3, 1))
TWO8 = ((0, 2), (0, 1), (2, 2), (2, 1))
STEPS = {("A", "x"): DIRECT4, ("A", "y"): TWO8, ("B", "y"): TWO8, ("B", "x"): CHAIN4}
STEPS_Z = TWO8


def around(n):
    out = [n // 2]
    for k in range(n // 2 - 1, 0, -1):
        out += [k, -k]
    return out + [0]


def gather_part(me, root, met, feat_ref, rows_ref, cols_ref, count_ref, codes_ref, xg_ref, masks_ref, tab_ref, at_ref, b_ref):
    for h in range(2):
        spread = jnp.broadcast_to(root[h : h + 1, :], (T, T)).T
        xg_ref[rows_of(me.row, h * T, T), :] = (spread * feat_ref[h * T : (h + 1) * T, :].astype(F32)).astype(BF16)
    met()
    plan = Plan()

    def leg(which, axis, o, d, b, h):
        n = NX if axis == "x" else NY
        first, size = part_rows(which, d, b + h == n // 2)
        piece = me.xy_piece(-d * b, o) if axis == "x" else me.xy_piece(o, -d * b)
        where = lambda: xg_ref.at[rows_of(piece, first, size), :]
        dev = me.at_xy(d * h, 0) if axis == "x" else me.at_xy(0, d * h)
        key = (which, axis, o, d, b + h)
        plan.message(key, (axis, d, h), size * 256, me.copier(where, where, dev))
        return key

    for which, one in (("A", "x"), ("B", "y")):
        for b, h in STEPS[which, one]:
            for d in (1, -1):
                need = [(which, one, 0, d, b)] if b else []
                plan.action(need, None, [leg(which, one, 0, d, b, h)])
    for which, one, two in (("A", "x", "y"), ("B", "y", "x")):
        n1 = NX if one == "x" else NY
        for o in around(n1)[::-1]:
            if o == 0:
                have = []
            elif o == n1 // 2:
                have = [(which, one, 0, 1, o), (which, one, 0, -1, o)]
            else:
                have = [(which, one, 0, -1 if o > 0 else 1, abs(o))]
            for b, h in STEPS[which, two]:
                for d in (1, -1):
                    need = [(which, two, o, d, b)] if b else have
                    plan.action(need, None, [leg(which, two, o, d, b, h)])

    def tables():
        lane = lax.broadcasted_iota(I32, (T, T), 1)
        sub = lax.broadcasted_iota(I32, (T, T), 0)
        out = []
        spread = [jnp.broadcast_to(v, (T, T)) for v in (rows_ref[...], cols_ref[...])]
        stood = [v.T for v in spread]
        for mine in (0, 1):
            key_l = spread[mine] * SLOTS + lane
            key_s = stood[mine] * SLOTS + sub
            rank = jnp.sum((key_s < key_l).astype(I32), axis=0, keepdims=True)
            hot = jnp.broadcast_to(rank, (T, T)).T == lane
            pick = lambda v: jnp.sum(jnp.where(hot, v, 0), axis=0, keepdims=True)
            order = pick(sub)
            target = pick(stood[mine])
            source = pick(stood[1 - mine])
            same = (target == pltpu.roll(target, 1, 1)) & (lane[:1] > 0)
            last = jnp.sum((stood[mine] <= lane).astype(I32), axis=0, keepdims=True) - 1
            has = jnp.sum((stood[mine] == lane).astype(I32), axis=0, keepdims=True)
            out += [order, source, same.astype(I32), jnp.maximum(last, 0), (has > 0).astype(I32)]
        for i, v in enumerate(out):
            tab_ref[i : i + 1, :] = v

    def codes_ready():
        live = lax.broadcasted_iota(I32, (SLOTS, T), 0) < count_ref[0, 0]
        a = codes_ref[:, :T] + 3
        a = jnp.where(a >= PRIME, a - PRIME, a)
        a = jnp.where(live, a, 0)
        at_ref[...] = a.astype(F32).T
        b = codes_ref[:, T:] + 1
        b_ref[...] = jnp.where(b >= PRIME, b - PRIME, b).astype(F32)

    def mask_group(g):
        at = at_ref[...]
        for u in range(8):
            s = g * 8 + u
            prod = at[:, u : u + 1] * b_ref[s : s + 1, :]
            near_q = (prod * (1.0 / PRIME) + ROUND) - ROUND
            left = prod - near_q * PRIME
            hit = (left >= 3.0) & (left < 67.0)
            masks_ref[s * T : (s + 1) * T, :] = jnp.where(hit, 1.0, 0.0).astype(BF16)
        at_ref[...] = pltpu.roll(at, T - 8, 1)

    plan.filler(codes_ready, 0.3)
    for g in range(SLOTS // 8):
        plan.filler(functools.partial(mask_group, g), 0.35)
    plan.filler(tables, 0.8)
    plan.run()
    return [plan]


UNROLL = 8


def tile_at(t):
    return pl.ds(t * T, T)


def product_part(forward, tab_ref, masks_ref, src_ref, out_ref, pre_ref):
    base = 0 if forward else 5

    def step(g, acc):
        for u in range(UNROLL):
            j = g * UNROLL + u
            mask = masks_ref[tile_at(tab_ref[base, j]), :]
            src = src_ref[tile_at(tab_ref[base + 1, j]), :]
            new = jnp.dot(mask, src, preferred_element_type=F32) if forward else jnp.dot(src, mask, preferred_element_type=F32)
            acc = acc * tab_ref[base + 2, j].astype(F32) + new
            pre_ref[tile_rows(j), :] = acc
        return acc

    lax.fori_loop(0, SLOTS // UNROLL, step, jnp.zeros((T, T), F32))

    def form(t):
        v = pre_ref[tile_at(tab_ref[base + 3, t]), :]
        out_ref[tile_rows(t), :] = (v * tab_ref[base + 4, t].astype(F32)).astype(BF16)

    return form


W1 = T // 2
WY = W1 // NY


def dense_part(
    me, root, form, rp_ref, weight_ref, bias_ref, cot_ref, hid_ref, gt_ref, gsum_ref,
    acc_ref, cs_ref, zs_ref, gl_ref, g1_ref, gz_ref, g2_ref, g3x_ref,
):
    core, mx, my = me.core, me.mx, me.my
    plan = Plan()
    offsets = around(NZ)
    chunks = [(c, c * T, T) for c in range(PIECE // T)]
    for c, first, size in chunks:
        for i, o in enumerate(offsets):
            theirs = me.z_piece(o, 1 - core)
            plan.message(
                ("c", o, c), ("c", 1), size * 256,
                me.copier(
                    functools.partial(lambda p, f, s: rp_ref.at[rows_of(p, f, s), :], theirs, first, size),
                    functools.partial(lambda f, s: cs_ref.at[pl.ds(f, s), :], i * PIECE + first, size),
                    me.other,
                ),
            )
            plan.action([], functools.partial(form, theirs * 2 + c), [("c", o, c)], 0.03)
    for c, _, _ in chunks:
        for o in offsets:
            plan.action([], functools.partial(form, me.z_piece(o, core) * 2 + c), (), 0.03)
    legs = {}
    base = 0
    for d in (1, -1):
        for b, h in STEPS_Z:
            for c, first, size in chunks:
                if b + h == NZ // 2:
                    first, size = half(first, size, d)
                piece = me.z_piece(d * (b + h), core)
                legs[d, b, h, c] = (base, first, size, piece)
                plan.message(
                    ("z", d, b, h, c), ("z", d, h), size * 256,
                    me.copier(
                        functools.partial(lambda p, f, s: acc_ref.at[rows_of(p, f, s), :], piece, first, size),
                        functools.partial(lambda b, s: zs_ref.at[pl.ds(b, s), :], base, size),
                        me.at_z(d * h),
                    ),
                )
                base += size

    def z_add(d, b, h, c, before):
        o = NZ // 2 if b + h == NZ // 2 else d * (b + h)
        _, first, size, piece = legs[d, b, h, c]
        given = [(cs_ref, offsets.index(o) * PIECE, 0, PIECE)] + [(zs_ref,) + legs[k][:3] for k in before]
        combine(acc_ref, rp_ref, piece, first, size, given)

    for c, _, _ in chunks:
        for b, h in sorted(STEPS_Z, key=lambda s: (-s[0], -s[1])):
            for d in (1, -1):
                before = [(d, b2, h2, c) for b2, h2 in STEPS_Z if b2 == b + h]
                deps = [("c", NZ // 2 if b + h == NZ // 2 else d * (b + h), c)] + [("z",) + k for k in before]
                plan.action(deps, functools.partial(z_add, d, b, h, c, before), [("z", d, b, h, c)], 0.06)
    plan.run()

    i0 = offsets.index(0)
    agg_sum = rp_ref[rows_of(me.col, 0, PIECE), :].astype(F32) + cs_ref[i0 * PIECE : (i0 + 1) * PIECE, :].astype(F32)
    for d in (1, -1):
        for b, h in STEPS_Z:
            if b == 0:
                got = [zs_ref[pl.ds(legs[d, b, h, c][0], size), :] for c, _, size in chunks]
                agg_sum = agg_sum + jnp.concatenate([g.astype(F32) for g in got], axis=0)
    spread = jnp.concatenate([jnp.broadcast_to(root[h : h + 1, :], (T, T)).T for h in range(2)], axis=0)
    aggregate = (spread * agg_sum).astype(BF16)
    weight = weight_ref[...]
    preact = jnp.dot(aggregate, weight, preferred_element_type=F32) + bias_ref[...]
    below = jnp.exp(jnp.minimum(preact, 0.0))
    hid_ref[...] = jnp.where(preact > 0, preact, below - 1.0).astype(BF16)
    grad_pre = cot_ref[...].astype(F32) * jnp.where(preact > 0, 1.0, below)
    grad_pre_b = grad_pre.astype(BF16)
    grad_agg_t = lax.dot_general(weight, grad_pre_b, (((1,), (1,)), ((), ())), preferred_element_type=F32)
    for h in range(2):
        gt_ref[rows_of(me.col, h * T, T), :] = (grad_agg_t[:, h * T : (h + 1) * T] * root[h : h + 1, :]).astype(BF16)

    plan2 = Plan()
    for c, first, size in chunks:
        for b, h in STEPS_Z:
            for d in (1, -1):
                f, n = half(first, size, d) if b + h == NZ // 2 else (first, size)
                piece = me.z_piece(-d * b, core)
                where = functools.partial(lambda p, f, s: gt_ref.at[rows_of(p, f, s), :], piece, f, n)
                plan2.message(("Z", d, b + h, c), ("z", d, h), n * 256, me.copier(where, where, me.at_z(d * h)))
                plan2.action([("Z", d, b, c)] if b else [], None, [("Z", d, b + h, c)])
    for c, first, size in chunks:
        for o in offsets:
            where = functools.partial(lambda p, f, s: gt_ref.at[rows_of(p, f, s), :], me.z_piece(o, core), first, size)
            plan2.message(("C", o, c), ("c", 1), size * 256, me.copier(where, where, me.other))
        plan2.action([], None, [("C", 0, c)])
        for k in range(1, NZ // 2 + 1):
            if k == NZ // 2:
                plan2.action([("Z", 1, k, c), ("Z", -1, k, c)], None, [("C", k, c)])
            else:
                for d in (1, -1):
                    plan2.action([("Z", d, k, c)], None, [("C", -d * k, c)])

    scale = 1.0 / math.sqrt(PIECE * NX * NY * NZ * 2)

    def grads():
        agg_t = aggregate.astype(F32).T.astype(BF16)
        gw = jnp.dot(agg_t, grad_pre_b, preferred_element_type=F32) * scale
        gb = jnp.sum(grad_pre, axis=0, keepdims=True) * scale
        gb8 = jnp.where(lax.broadcasted_iota(I32, (8, T), 0) == 0, gb, 0.0)
        for k in range(2):
            gl_ref[k * 72 : k * 72 + W1, :] = gw[k * W1 : (k + 1) * W1, :]
            gl_ref[k * 72 + W1 : (k + 1) * 72, :] = gb8

    plan2.message(
        ("G", 1), ("c", 1), 72 * 512,
        me.copier(lambda: gl_ref.at[slots_of(1 - core, 72), :], lambda: g1_ref.at[:, :], me.other),
    )
    plan2.action([], grads, [("G", 1)], 0.5)
    g2 = []
    for o in range(1, NY):
        g2.append(("G2", o))
        plan2.message(
            ("G2", o), ("gy", o), 16 * 512,
            me.copier(
                functools.partial(lambda o: gz_ref.at[slots_of(lax.rem(my + o, NY), 16), :], o),
                lambda: g2_ref.at[slots_of(my, 16), :],
                me.at_xy(0, o),
            ),
        )

    def after_chip():
        total = gl_ref[slots_of(core, 72), :] + g1_ref[...]
        for y in range(NY):
            gz_ref[y * 16 : y * 16 + 8, :] = total[y * WY : (y + 1) * WY, :]
            gz_ref[y * 16 + 8 : y * 16 + 16, :] = total[W1 : W1 + 8, :]
        g2_ref[slots_of(my, 16), :] = gz_ref[slots_of(my, 16), :]

    plan2.action([("G", 1)], after_chip, g2, 0.2)
    own_x = lambda: g3x_ref.at[slots_of(mx, 16), :]
    g3x = []
    for o in range(1, NX):
        g3x.append(("G3x", o))
        plan2.message(("G3x", o), ("gx", o), 16 * 512, me.copier(own_x, own_x, me.at_xy(o, 0)))

    def after_y():
        g3x_ref[slots_of(mx, 16), :] = total_of(g2_ref, NY)

    plan2.action(g2, after_y, g3x, 0.1)

    def after_x():
        gsum_ref[...] = total_of(g3x_ref, NX)

    plan2.action(g3x, after_x, (), 0.05)
    plan2.run()
    return [plan, plan2]


def total_of(ref, n):
    v = ref[0:16, :]
    for i in range(1, n):
        v = v + ref[i * 16 : (i + 1) * 16, :]
    return v


def scatter_part(me, root, form, cp_ref, gsum_ref, gf_ref, gw_ref, gb_ref, acc_ref, sum_ref, g3_ref, g4_ref, yx_ref):
    core, mz, my = me.core, me.mz, me.my
    plan = Plan()
    slot_rows = [0]

    def leg(which, axis, o, d, b, h, src):
        n = NX if axis == "x" else NY
        first, size = part_rows(which, d, b + h == n // 2)
        piece = me.xy_piece(d * (b + h), o) if axis == "x" else me.xy_piece(o, d * (b + h))
        base = slot_rows[0]
        slot_rows[0] += size
        dev = me.at_xy(d * h, 0) if axis == "x" else me.at_xy(0, d * h)
        key = ("s", which, axis, o, d, b, h)
        plan.message(
            key, (axis, d, h), size * 256,
            me.copier(
                lambda: src.at[rows_of(piece, first, size), :], lambda: sum_ref.at[pl.ds(base, size), :], dev
            ),
        )
        at = (d * (b + h), o) if axis == "x" else (o, d * (b + h))
        return dict(key=key, base=base, first=first, size=size, piece=piece, at=at)

    def given(*legs):
        return [(sum_ref, e["base"], e["first"], e["size"]) for e in legs]

    def adder(leg, *others):
        return lambda: combine(acc_ref, cp_ref, leg["piece"], leg["first"], leg["size"], given(*others))

    finals = {}
    late = []
    first_sends = []
    for which, one, two in (("A", "y", "x"), ("B", "x", "y")):
        n2 = NX if two == "x" else NY
        done = {}
        steps = sorted(STEPS[which, one], key=lambda s: (-s[0], -s[1]))
        for o in around(n2):
            done[o] = []
            for d in (1, -1):
                made = {}
                for b, h in steps:
                    prev = [made[k] for k in made if k[0] == b + h]
                    now = made[b, h] = leg(which, one, o, d, b, h, acc_ref if prev else cp_ref)
                    if prev:
                        late.append(([e["key"] for e in prev], adder(now, *prev), [now["key"]], 0.06))
                    else:
                        first_sends.append((b, now))
                    if b == 0:
                        done[o].append(now)
        finals[which] = list(done[0])
        for d in (1, -1):
            made = {}
            for b, h in sorted(STEPS[which, two], key=lambda s: (-s[0], -s[1])):
                prev = [made[k] for k in made if k[0] == b + h]
                now = made[b, h] = leg(which, two, 0, d, b, h, acc_ref)
                more = done[n2 // 2 if b + h == n2 // 2 else d * (b + h)] + prev
                late.append(([e["key"] for e in more], adder(now, *more), [now["key"]], 0.08))
                if b == 0:
                    finals[which].append(now)
    formed = []

    def form_rows(leg):
        x, y = leg["at"]
        for h in range(2):
            if leg["first"] < (h + 1) * T and leg["first"] + leg["size"] > h * T and (x % NX, y % NY, h) not in formed:
                formed.append((x % NX, y % NY, h))
                form(me.xy_piece(x % NX, y % NY) * 2 + h)

    for _, leg_now in sorted(first_sends, key=lambda e: -e[0]):
        plan.action([], functools.partial(form_rows, leg_now), [leg_now["key"]], 0.04)
    for x in range(NX):
        for y in range(NY):
            plan.action([], functools.partial(form_rows, dict(at=(x, y), first=0, size=PIECE)), (), 0.04)
    for deps, fn, sends, cost in late:
        plan.action(deps, fn, sends, cost)

    def ride(tag, n, dev, where, size):
        keys = []
        for o in range(1, n):
            keys.append((tag, o))
            plan.message((tag, o), (tag, o), size * 512, me.copier(where, where, dev(o)))
        return keys

    g3z = ride("G3z", NZ, me.at_z, lambda: g3_ref.at[slots_of(mz, 16), :], 16)

    def start_z():
        g3_ref[slots_of(mz, 16), :] = gsum_ref[...]

    plan.action([], start_z, g3z, 0.02)
    own_w = lambda: pl.ds(pl.multiple_of(core * W1 + my * WY, 8), WY)
    g4 = ride("G4", NY, lambda o: me.at_xy(0, o), lambda: g4_ref.at[own_w(), :], WY)

    def after_z():
        v = total_of(g3_ref, NZ)
        gb_ref[...] = v[8:9, :]
        g4_ref[own_w(), :] = v[0:8, :]

    plan.action(g3z, after_z, g4, 0.05)
    half_w = lambda: g4_ref.at[slots_of(core, W1), :]
    plan.message(("G5", 0), ("c", 1), W1 * 512, me.copier(half_w, half_w, me.other))
    plan.action(g4, None, [("G5", 0)])

    def give_weight():
        gw_ref[...] = g4_ref[...]

    plan.action([("G5", 0)], give_weight, (), 0.05)
    plan.run()

    yx_ref[...] = cp_ref[rows_of(me.row, 0, PIECE), :].astype(F32)
    for e in finals["A"] + finals["B"]:
        at = slice(e["first"], e["first"] + e["size"])
        yx_ref[at, :] = yx_ref[at, :] + sum_ref[pl.ds(e["base"], e["size"]), :].astype(F32)
    for h in range(2):
        v = yx_ref[h * T : (h + 1) * T, :] * root[h : h + 1, :]
        gf_ref[h * T : (h + 1) * T, :] = v.T.astype(BF16)
    return [plan]


COPIES = 242
ROW_NODES = PIECE * NZ * 2
COL_NODES = PIECE * NX * NY


def body(
    feat_ref, deg_ref, weight_ref, bias_ref, cot_ref, rows_ref, cols_ref, count_ref, codes_ref,
    hid_ref, gf_ref, gw_ref, gb_ref,
    xg_ref, masks_ref, tab_ref, at_ref, b_ref, pre_ref, rp_ref, racc_ref, cs_ref, zs_ref, gt_ref, cp_ref, cacc_ref,
    sum_ref, gsum_ref, gl_ref, g1_ref, gz_ref, g2_ref, g3_ref, g3x_ref, g4_ref, yx_ref,
    tab_s, tab_sem, send_sem, recv_sem,
):
    me = Place(send_sem, recv_sem)
    met = me.enter(
        [me.at_xy(o, 0) for o in (1, 2, 3)]
        + [me.at_xy(0, o) for o in (1, 2, -2, -1)]
        + [me.at_z(o) for o in (1, 2, -2, -1)]
        + [me.other]
    )
    root = lax.rsqrt(deg_ref[...].astype(F32))
    tab_ref[...] = jnp.zeros_like(tab_ref)
    plans = gather_part(
        me, root, met, feat_ref, rows_ref, cols_ref, count_ref, codes_ref, xg_ref, masks_ref, tab_ref, at_ref, b_ref
    )
    moved = pltpu.make_async_copy(tab_ref, tab_s, tab_sem)
    moved.start()
    moved.wait()
    form = product_part(True, tab_s, masks_ref, xg_ref, rp_ref, pre_ref)
    plans += dense_part(
        me, root, form, rp_ref, weight_ref, bias_ref, cot_ref, hid_ref, gt_ref, gsum_ref,
        racc_ref, cs_ref, zs_ref, gl_ref, g1_ref, gz_ref, g2_ref, g3x_ref,
    )
    form = product_part(False, tab_s, masks_ref, gt_ref, cp_ref, pre_ref)
    plans += scatter_part(
        me, root, form, cp_ref, gsum_ref, gf_ref, gw_ref, gb_ref, cacc_ref, sum_ref, g3_ref, g4_ref, yx_ref
    )
    for plan in plans:
        plan.drain()


def local(features, degree, weight, bias, cotangent, tile_rows, tile_cols, tile_count, tile_codes):
    vmem = pl.BlockSpec(memory_space=pltpu.VMEM)
    smem = pl.BlockSpec(memory_space=pltpu.SMEM)
    hidden, grad_features, grad_weight, grad_bias = pl.pallas_call(
        body,
        out_shape=(
            jax.ShapeDtypeStruct((PIECE, T), BF16),
            jax.ShapeDtypeStruct((PIECE, T), BF16),
            jax.ShapeDtypeStruct((T, T), F32),
            jax.ShapeDtypeStruct((1, T), F32),
        ),
        in_specs=[vmem] * 7 + [smem, vmem],
        out_specs=(vmem,) * 4,
        scratch_shapes=[
            pltpu.VMEM((COL_NODES, T), BF16),
            pltpu.VMEM((SLOTS * T, T), BF16),
            pltpu.VMEM((16, T), I32),
            pltpu.VMEM((T, SLOTS), F32),
            pltpu.VMEM((SLOTS, T), F32),
            pltpu.VMEM((SLOTS * T, T), F32),
            pltpu.VMEM((ROW_NODES, T), BF16),
            pltpu.VMEM((ROW_NODES, T), BF16),
            pltpu.VMEM((PIECE * NZ, T), BF16),
            pltpu.VMEM((PIECE * (NZ - 1), T), BF16),
            pltpu.VMEM((ROW_NODES, T), BF16),
            pltpu.VMEM((COL_NODES, T), BF16),
            pltpu.VMEM((COL_NODES, T), BF16),
            pltpu.VMEM((COL_NODES - PIECE, T), BF16),
            pltpu.VMEM((16, T), F32),
            pltpu.VMEM((144, T), F32),
            pltpu.VMEM((72, T), F32),
            pltpu.VMEM((16 * NY, T), F32),
            pltpu.VMEM((16 * NY, T), F32),
            pltpu.VMEM((16 * NZ, T), F32),
            pltpu.VMEM((16 * NX, T), F32),
            pltpu.VMEM((T, T), F32),
            pltpu.VMEM((PIECE, T), F32),
            pltpu.SMEM((16, T), I32),
            pltpu.SemaphoreType.DMA,
            pltpu.SemaphoreType.DMA((COPIES,)),
            pltpu.SemaphoreType.DMA((COPIES,)),
        ],
        compiler_params=pltpu.CompilerParams(collective_id=0, has_side_effects=True),
        name="layer",
    )(
        features,
        degree.reshape(2, T),
        weight,
        bias.reshape(1, T),
        cotangent,
        tile_rows.reshape(1, SLOTS),
        tile_cols.reshape(1, SLOTS),
        tile_count.reshape(1, 1),
        tile_codes.reshape(SLOTS, 2 * T),
    )
    return hidden, grad_features, grad_weight, grad_bias.reshape(T)


def solution(mesh):
    placed = (
        P(("row", "col"), None),
        P(("row", "col")),
        P(),
        P(),
        P(("row", "col"), None),
        P("row", "col", None),
        P("row", "col", None),
        P("row", "col", None),
        P("row", "col", None, None),
    )
    return jax.shard_map(
        local,
        mesh=mesh,
        in_specs=placed,
        out_specs=(P(("row", "col"), None), P(("row", "col"), None), P(), P()),
        check_vma=False,
    )
```

```python
import functools
import math

import jax
import jax.numpy as jnp
from jax import lax
from jax.experimental import pallas as pl
from jax.experimental.pallas import tpu as pltpu
from jax.sharding import PartitionSpec as P

MESH = pl.DeviceIdType.MESH
F32 = jnp.float32
BF16 = jnp.bfloat16
I32 = jnp.int32

NX, NY, NZ = 4, 8, 8
PIECE = 256
T = 128
SLOTS = 128
PRIME = 4093
ROUND = 12582912.0
CUT = 96

WIRE = 46e3
CORE_WIRE = 250e3
HOP = 2.5
HOP_MORE = 0.5
CORE_HOP = 0.95


class Plan:
    def __init__(self):
        self.copies = {}
        self.actions = []
        self.fillers = []

    def message(self, key, link, nbytes, make):
        self.copies[key] = [link, nbytes, make, None]

    def action(self, deps, fn, sends=(), cost=0.03):
        self.actions.append((tuple(deps), fn, tuple(sends), cost))

    def filler(self, fn, cost):
        self.fillers.append((fn, cost))

    def run(self, leave=()):
        now = 0.0
        free = {}
        arrival = {}
        todo = list(self.actions)
        fill = list(self.fillers)
        waited = set()
        while todo:
            best, best_at = None, None
            for item in todo:
                if all(d in arrival for d in item[0]):
                    at = max([now] + [arrival[d] for d in item[0]])
                    if best is None or at < best_at - 1e-9:
                        best, best_at = item, at
            if fill and best_at > now + 0.1:
                fn, cost = fill.pop(0)
                fn()
                now += cost
                continue
            deps, fn, sends, cost = best
            todo.remove(best)
            for d in sorted(deps, key=lambda d: arrival[d]):
                if d not in waited:
                    waited.add(d)
                    self.copies[d][3].wait_recv()
            now = best_at
            if fn is not None:
                fn()
                now += cost
            for key in sends:
                link, nbytes, make, _ = self.copies[key]
                copy = make()
                self.copies[key][3] = copy
                copy.start()
                hops = link[2] if len(link) > 2 else 1
                wire, hop = (CORE_WIRE, CORE_HOP) if link[0] == "c" else (WIRE, HOP + HOP_MORE * (hops - 1))
                link = link[:2]
                free[link] = max(free.get(link, 0.0), now) + nbytes * hops / wire
                arrival[key] = free[link] + hop
        for fn, cost in fill:
            fn()
        for key, item in self.copies.items():
            if key not in waited and key not in leave:
                item[3].wait_recv()

    def drain(self):
        for item in self.copies.values():
            item[3].wait_send()


class Place:
    def __init__(self, send_sem, recv_sem):
        self.row = row = lax.axis_index("row")
        self.col = col = lax.axis_index("col")
        self.mx, self.my = row // NY, row % NY
        self.mz, self.core = col // 2, col % 2
        self.other = (row, self.mz * 2 + (1 - self.core))
        self.send_sem, self.recv_sem = send_sem, recv_sem
        self.used = 0

    def xy_piece(self, x, y):
        return lax.rem(self.mx + x + NX, NX) * NY + lax.rem(self.my + y + NY, NY)

    def z_piece(self, z, k):
        return lax.rem(self.mz + z + NZ, NZ) * 2 + k

    def at_xy(self, x, y):
        return (self.xy_piece(x, y), self.col)

    def at_z(self, z):
        return (self.row, self.z_piece(z, self.core))

    def copier(self, src, dst, dev):
        i = self.used
        self.used += 1

        def make():
            return pltpu.make_async_remote_copy(
                src_ref=src(), dst_ref=dst(), send_sem=self.send_sem.at[i], recv_sem=self.recv_sem.at[i],
                device_id=dev, device_id_type=MESH,
            )

        return make

    def enter(self, peers):
        barrier = pltpu.get_barrier_semaphore()
        for dev in peers:
            pl.semaphore_signal(barrier, inc=1, device_id=dev, device_id_type=MESH)

        def met():
            pl.semaphore_wait(barrier, len(peers))

        return met


def rows_of(start, first, size):
    return pl.ds(pl.multiple_of(start * PIECE + first, 16), size)


def tile_rows(t):
    return pl.ds(pl.multiple_of(t * T, T), T)


def slots_of(i, n):
    return pl.ds(pl.multiple_of(i * n, 8), n)


PARTS = {"A": (0, CUT), "B": (CUT, PIECE - CUT)}


def half(first, size, d):
    return (first, size // 2) if d > 0 else (first + size // 2, size // 2)


def part_rows(which, d, last):
    first, size = PARTS[which]
    return half(first, size, d) if last else (first, size)


def combine(dst, src, piece, first, size, given):
    whole = all(n >= size for _, _, _, n in given)
    blocks = [(first, size)] if whole else [half(first, size, 1), half(first, size, -1)]
    for f, n in blocks:
        v = src[rows_of(piece, f, n), :].astype(F32)
        for ref, base, gf, gn in given:
            if gf <= f and f + n <= gf + gn:
                v = v + ref[pl.ds(base + f - gf, n), :].astype(F32)
        dst[rows_of(piece, f, n), :] = v.astype(BF16)


DIRECT4 = ((0, 1), (0, 2))
TWO8 = ((0, 2), (0, 1), (2, 2), (2, 1))
STEPS = {("A", "x"): DIRECT4, ("A", "y"): TWO8, ("B", "y"): TWO8, ("B", "x"): DIRECT4}
STEPS_Z = TWO8


def around(n):
    out = [n // 2]
    for k in range(n // 2 - 1, 0, -1):
        out += [k, -k]
    return out + [0]


def gather_part(me, root, met, feat_ref, rows_ref, cols_ref, count_ref, codes_ref, xg_ref, masks_ref, tab_ref, at_ref, b_ref):
    for h in range(2):
        spread = jnp.broadcast_to(root[h : h + 1, :], (T, T)).T
        xg_ref[rows_of(me.row, h * T, T), :] = (spread * feat_ref[h * T : (h + 1) * T, :].astype(F32)).astype(BF16)
    met()
    plan = Plan()

    def leg(which, axis, o, d, b, h):
        n = NX if axis == "x" else NY
        first, size = part_rows(which, d, b + h == n // 2)
        piece = me.xy_piece(-d * b, o) if axis == "x" else me.xy_piece(o, -d * b)
        where = lambda: xg_ref.at[rows_of(piece, first, size), :]
        dev = me.at_xy(d * h, 0) if axis == "x" else me.at_xy(0, d * h)
        key = (which, axis, o, d, b + h)
        plan.message(key, (axis, d, h), size * 256, me.copier(where, where, dev))
        return key

    for which, one in (("A", "x"), ("B", "y")):
        for b, h in STEPS[which, one]:
            for d in (1, -1):
                need = [(which, one, 0, d, b)] if b else []
                plan.action(need, None, [leg(which, one, 0, d, b, h)])
    for which, one, two in (("A", "x", "y"), ("B", "y", "x")):
        n1 = NX if one == "x" else NY
        for o in around(n1)[::-1]:
            if o == 0:
                have = []
            elif o == n1 // 2:
                have = [(which, one, 0, 1, o), (which, one, 0, -1, o)]
            else:
                have = [(which, one, 0, -1 if o > 0 else 1, abs(o))]
            for b, h in STEPS[which, two]:
                for d in (1, -1):
                    need = [(which, two, o, d, b)] if b else have
                    plan.action(need, None, [leg(which, two, o, d, b, h)])

    def tables():
        lane = lax.broadcasted_iota(I32, (T, T), 1)
        sub = lax.broadcasted_iota(I32, (T, T), 0)
        out = []
        spread = [jnp.broadcast_to(v, (T, T)) for v in (rows_ref[...], cols_ref[...])]
        stood = [v.T for v in spread]
        for mine in (0, 1):
            key_l = spread[mine] * SLOTS + lane
            key_s = stood[mine] * SLOTS + sub
            rank = jnp.sum((key_s < key_l).astype(I32), axis=0, keepdims=True)
            hot = jnp.broadcast_to(rank, (T, T)).T == lane
            pick = lambda v: jnp.sum(jnp.where(hot, v, 0), axis=0, keepdims=True)
            order = pick(sub)
            target = pick(stood[mine])
            source = pick(stood[1 - mine])
            same = (target == pltpu.roll(target, 1, 1)) & (lane[:1] > 0)
            last = jnp.sum((stood[mine] <= lane).astype(I32), axis=0, keepdims=True) - 1
            has = jnp.sum((stood[mine] == lane).astype(I32), axis=0, keepdims=True)
            out += [order, source, same.astype(I32), jnp.maximum(last, 0), (has > 0).astype(I32)]
        for i, v in enumerate(out):
            tab_ref[i : i + 1, :] = v

    def codes_ready():
        live = lax.broadcasted_iota(I32, (SLOTS, T), 0) < count_ref[0, 0]
        a = codes_ref[:, :T] + 3
        a = jnp.where(a >= PRIME, a - PRIME, a)
        a = jnp.where(live, a, 0)
        at_ref[...] = a.astype(F32).T
        b = codes_ref[:, T:] + 1
        b_ref[...] = jnp.where(b >= PRIME, b - PRIME, b).astype(F32)

    def mask_group(g):
        at = at_ref[...]
        for u in range(8):
            s = g * 8 + u
            prod = at[:, u : u + 1] * b_ref[s : s + 1, :]
            near_q = (prod * (1.0 / PRIME) + ROUND) - ROUND
            left = prod - near_q * PRIME
            hit = (left >= 3.0) & (left < 67.0)
            masks_ref[s * T : (s + 1) * T, :] = jnp.where(hit, 1.0, 0.0).astype(BF16)
        at_ref[...] = pltpu.roll(at, T - 8, 1)

    plan.filler(codes_ready, 0.3)
    for g in range(SLOTS // 8):
        plan.filler(functools.partial(mask_group, g), 0.35)
    plan.filler(tables, 0.8)
    plan.run()
    return [plan]


UNROLL = 8


def tile_at(t):
    return pl.ds(t * T, T)


def product_part(forward, tab_ref, masks_ref, src_ref, out_ref, pre_ref):
    base = 0 if forward else 5

    def step(g, acc):
        for u in range(UNROLL):
            j = g * UNROLL + u
            mask = masks_ref[tile_at(tab_ref[base, j]), :]
            src = src_ref[tile_at(tab_ref[base + 1, j]), :]
            new = jnp.dot(mask, src, preferred_element_type=F32) if forward else jnp.dot(src, mask, preferred_element_type=F32)
            acc = acc * tab_ref[base + 2, j].astype(F32) + new
            pre_ref[tile_rows(j), :] = acc
        return acc

    lax.fori_loop(0, SLOTS // UNROLL, step, jnp.zeros((T, T), F32))

    def form(t):
        v = pre_ref[tile_at(tab_ref[base + 3, t]), :]
        out_ref[tile_rows(t), :] = (v * tab_ref[base + 4, t].astype(F32)).astype(BF16)

    return form


W1 = T // 2
WY = W1 // NY


def dense_part(
    me, root, form, rp_ref, weight_ref, bias_ref, cot_ref, hid_ref, gt_ref, gsum_ref,
    acc_ref, cs_ref, zs_ref, gl_ref, g1_ref, gz_ref, g2_ref, g3x_ref,
):
    core, mx, my = me.core, me.mx, me.my
    plan = Plan()
    offsets = around(NZ)
    chunks = [(c, c * T, T) for c in range(PIECE // T)]
    for c, first, size in chunks:
        for i, o in enumerate(offsets):
            theirs = me.z_piece(o, 1 - core)
            plan.message(
                ("c", o, c), ("c", 1), size * 256,
                me.copier(
                    functools.partial(lambda p, f, s: rp_ref.at[rows_of(p, f, s), :], theirs, first, size),
                    functools.partial(lambda f, s: cs_ref.at[pl.ds(f, s), :], i * PIECE + first, size),
                    me.other,
                ),
            )
            plan.action([], functools.partial(form, theirs * 2 + c), [("c", o, c)], 0.03)
    for c, _, _ in chunks:
        for o in offsets:
            plan.action([], functools.partial(form, me.z_piece(o, core) * 2 + c), (), 0.03)
    legs = {}
    base = 0
    for d in (1, -1):
        for b, h in STEPS_Z:
            for c, first, size in chunks:
                if b + h == NZ // 2:
                    first, size = half(first, size, d)
                piece = me.z_piece(d * (b + h), core)
                legs[d, b, h, c] = (base, first, size, piece)
                plan.message(
                    ("z", d, b, h, c), ("z", d, h), size * 256,
                    me.copier(
                        functools.partial(lambda p, f, s: acc_ref.at[rows_of(p, f, s), :], piece, first, size),
                        functools.partial(lambda b, s: zs_ref.at[pl.ds(b, s), :], base, size),
                        me.at_z(d * h),
                    ),
                )
                base += size

    def z_add(d, b, h, c, before):
        o = NZ // 2 if b + h == NZ // 2 else d * (b + h)
        _, first, size, piece = legs[d, b, h, c]
        given = [(cs_ref, offsets.index(o) * PIECE, 0, PIECE)] + [(zs_ref,) + legs[k][:3] for k in before]
        combine(acc_ref, rp_ref, piece, first, size, given)

    for c, _, _ in chunks:
        for b, h in sorted(STEPS_Z, key=lambda s: (-s[0], -s[1])):
            for d in (1, -1):
                before = [(d, b2, h2, c) for b2, h2 in STEPS_Z if b2 == b + h]
                deps = [("c", NZ // 2 if b + h == NZ // 2 else d * (b + h), c)] + [("z",) + k for k in before]
                plan.action(deps, functools.partial(z_add, d, b, h, c, before), [("z", d, b, h, c)], 0.06)
    plan.run()

    i0 = offsets.index(0)
    agg_sum = rp_ref[rows_of(me.col, 0, PIECE), :].astype(F32) + cs_ref[i0 * PIECE : (i0 + 1) * PIECE, :].astype(F32)
    for d in (1, -1):
        for b, h in STEPS_Z:
            if b == 0:
                got = [zs_ref[pl.ds(legs[d, b, h, c][0], size), :] for c, _, size in chunks]
                agg_sum = agg_sum + jnp.concatenate([g.astype(F32) for g in got], axis=0)
    spread = jnp.concatenate([jnp.broadcast_to(root[h : h + 1, :], (T, T)).T for h in range(2)], axis=0)
    aggregate = (spread * agg_sum).astype(BF16)
    weight = weight_ref[...]
    preact = jnp.dot(aggregate, weight, preferred_element_type=F32) + bias_ref[...]
    below = jnp.exp(jnp.minimum(preact, 0.0))
    hid_ref[...] = jnp.where(preact > 0, preact, below - 1.0).astype(BF16)
    grad_pre = cot_ref[...].astype(F32) * jnp.where(preact > 0, 1.0, below)
    grad_pre_b = grad_pre.astype(BF16)
    grad_agg_t = lax.dot_general(weight, grad_pre_b, (((1,), (1,)), ((), ())), preferred_element_type=F32)
    for h in range(2):
        gt_ref[rows_of(me.col, h * T, T), :] = (grad_agg_t[:, h * T : (h + 1) * T] * root[h : h + 1, :]).astype(BF16)

    plan2 = Plan()
    for c, first, size in chunks:
        for b, h in STEPS_Z:
            for d in (1, -1):
                f, n = half(first, size, d) if b + h == NZ // 2 else (first, size)
                piece = me.z_piece(-d * b, core)
                where = functools.partial(lambda p, f, s: gt_ref.at[rows_of(p, f, s), :], piece, f, n)
                plan2.message(("Z", d, b + h, c), ("z", d, h), n * 256, me.copier(where, where, me.at_z(d * h)))
                plan2.action([("Z", d, b, c)] if b else [], None, [("Z", d, b + h, c)])
    for c, first, size in chunks:
        for o in offsets:
            where = functools.partial(lambda p, f, s: gt_ref.at[rows_of(p, f, s), :], me.z_piece(o, core), first, size)
            plan2.message(("C", o, c), ("c", 1), size * 256, me.copier(where, where, me.other))
        plan2.action([], None, [("C", 0, c)])
        for k in range(1, NZ // 2 + 1):
            if k == NZ // 2:
                plan2.action([("Z", 1, k, c), ("Z", -1, k, c)], None, [("C", k, c)])
            else:
                for d in (1, -1):
                    plan2.action([("Z", d, k, c)], None, [("C", -d * k, c)])

    scale = 1.0 / math.sqrt(PIECE * NX * NY * NZ * 2)

    def grads():
        agg_t = aggregate.astype(F32).T.astype(BF16)
        gw = jnp.dot(agg_t, grad_pre_b, preferred_element_type=F32) * scale
        gb = jnp.sum(grad_pre, axis=0, keepdims=True) * scale
        gb8 = jnp.where(lax.broadcasted_iota(I32, (8, T), 0) == 0, gb, 0.0)
        for k in range(2):
            gl_ref[k * 72 : k * 72 + W1, :] = gw[k * W1 : (k + 1) * W1, :]
            gl_ref[k * 72 + W1 : (k + 1) * 72, :] = gb8

    plan2.message(
        ("G", 1), ("c", 1), 72 * 512,
        me.copier(lambda: gl_ref.at[slots_of(1 - core, 72), :], lambda: g1_ref.at[:, :], me.other),
    )
    plan2.action([], grads, [("G", 1)], 0.5)
    g2 = []
    for o in range(1, NY):
        g2.append(("G2", o))
        plan2.message(
            ("G2", o), ("gy", o), 16 * 512,
            me.copier(
                functools.partial(lambda o: gz_ref.at[slots_of(lax.rem(my + o, NY), 16), :], o),
                lambda: g2_ref.at[slots_of(my, 16), :],
                me.at_xy(0, o),
            ),
        )

    def after_chip():
        total = gl_ref[slots_of(core, 72), :] + g1_ref[...]
        for y in range(NY):
            gz_ref[y * 16 : y * 16 + 8, :] = total[y * WY : (y + 1) * WY, :]
            gz_ref[y * 16 + 8 : y * 16 + 16, :] = total[W1 : W1 + 8, :]
        g2_ref[slots_of(my, 16), :] = gz_ref[slots_of(my, 16), :]

    plan2.action([("G", 1)], after_chip, g2, 0.2)
    own_x = lambda: g3x_ref.at[slots_of(mx, 16), :]
    g3x = []
    for o in range(1, NX):
        g3x.append(("G3x", o))
        plan2.message(("G3x", o), ("gx", o), 16 * 512, me.copier(own_x, own_x, me.at_xy(o, 0)))

    def after_y():
        g3x_ref[slots_of(mx, 16), :] = total_of(g2_ref, NY)

    plan2.action(g2, after_y, g3x, 0.1)

    def after_x():
        gsum_ref[...] = total_of(g3x_ref, NX)

    plan2.action(g3x, after_x, (), 0.05)
    plan2.run()
    return [plan, plan2]


def total_of(ref, n):
    v = ref[0:16, :]
    for i in range(1, n):
        v = v + ref[i * 16 : (i + 1) * 16, :]
    return v


def scatter_part(me, root, form, cp_ref, gsum_ref, gf_ref, gw_ref, gb_ref, acc_ref, sum_ref, g3_ref, g4_ref, yx_ref):
    core, mz, my = me.core, me.mz, me.my
    plan = Plan()
    slot_rows = [0]

    def leg(which, axis, o, d, b, h, src):
        n = NX if axis == "x" else NY
        first, size = part_rows(which, d, b + h == n // 2)
        piece = me.xy_piece(d * (b + h), o) if axis == "x" else me.xy_piece(o, d * (b + h))
        base = slot_rows[0]
        slot_rows[0] += size
        dev = me.at_xy(d * h, 0) if axis == "x" else me.at_xy(0, d * h)
        key = ("s", which, axis, o, d, b, h)
        plan.message(
            key, (axis, d, h), size * 256,
            me.copier(
                lambda: src.at[rows_of(piece, first, size), :], lambda: sum_ref.at[pl.ds(base, size), :], dev
            ),
        )
        at = (d * (b + h), o) if axis == "x" else (o, d * (b + h))
        return dict(key=key, base=base, first=first, size=size, piece=piece, at=at)

    def given(*legs):
        return [(sum_ref, e["base"], e["first"], e["size"]) for e in legs]

    def adder(leg, *others):
        return lambda: combine(acc_ref, cp_ref, leg["piece"], leg["first"], leg["size"], given(*others))

    finals = {}
    late = []
    first_sends = []
    for which, one, two in (("A", "y", "x"), ("B", "x", "y")):
        n2 = NX if two == "x" else NY
        done = {}
        steps = sorted(STEPS[which, one], key=lambda s: (-s[0], -s[1]))
        for o in around(n2):
            done[o] = []
            for d in (1, -1):
                made = {}
                for b, h in steps:
                    prev = [made[k] for k in made if k[0] == b + h]
                    now = made[b, h] = leg(which, one, o, d, b, h, acc_ref if prev else cp_ref)
                    if prev:
                        late.append(([e["key"] for e in prev], adder(now, *prev), [now["key"]], 0.06))
                    else:
                        first_sends.append((b, now))
                    if b == 0:
                        done[o].append(now)
        finals[which] = list(done[0])
        for d in (1, -1):
            made = {}
            for b, h in sorted(STEPS[which, two], key=lambda s: (-s[0], -s[1])):
                prev = [made[k] for k in made if k[0] == b + h]
                now = made[b, h] = leg(which, two, 0, d, b, h, acc_ref)
                more = done[n2 // 2 if b + h == n2 // 2 else d * (b + h)] + prev
                late.append(([e["key"] for e in more], adder(now, *more), [now["key"]], 0.08))
                if b == 0:
                    finals[which].append(now)
    formed = []

    def form_rows(leg):
        x, y = leg["at"]
        for h in range(2):
            if leg["first"] < (h + 1) * T and leg["first"] + leg["size"] > h * T and (x % NX, y % NY, h) not in formed:
                formed.append((x % NX, y % NY, h))
                form(me.xy_piece(x % NX, y % NY) * 2 + h)

    for _, leg_now in sorted(first_sends, key=lambda e: -e[0]):
        plan.action([], functools.partial(form_rows, leg_now), [leg_now["key"]], 0.04)
    for x in range(NX):
        for y in range(NY):
            plan.action([], functools.partial(form_rows, dict(at=(x, y), first=0, size=PIECE)), (), 0.04)
    for deps, fn, sends, cost in late:
        plan.action(deps, fn, sends, cost)

    def ride(tag, n, dev, where, size):
        keys = []
        for o in range(1, n):
            keys.append((tag, o))
            plan.message((tag, o), (tag, o), size * 512, me.copier(where, where, dev(o)))
        return keys

    g3z = ride("G3z", NZ, me.at_z, lambda: g3_ref.at[slots_of(mz, 16), :], 16)

    def start_z():
        g3_ref[slots_of(mz, 16), :] = gsum_ref[...]

    plan.action([], start_z, g3z, 0.02)
    own_w = lambda: pl.ds(pl.multiple_of(core * W1 + my * WY, 8), WY)
    g4 = ride("G4", NY, lambda o: me.at_xy(0, o), lambda: g4_ref.at[own_w(), :], WY)

    def after_z():
        v = total_of(g3_ref, NZ)
        gb_ref[...] = v[8:9, :]
        g4_ref[own_w(), :] = v[0:8, :]

    plan.action(g3z, after_z, g4, 0.05)
    half_w = lambda: g4_ref.at[slots_of(core, W1), :]
    plan.message(("G5", 0), ("c", 1), W1 * 512, me.copier(half_w, half_w, me.other))
    plan.action(g4, None, [("G5", 0)])

    def give_weight():
        gw_ref[...] = g4_ref[...]

    plan.action([("G5", 0)], give_weight, (), 0.05)
    plan.run()

    yx_ref[...] = cp_ref[rows_of(me.row, 0, PIECE), :].astype(F32)
    for e in finals["A"] + finals["B"]:
        at = slice(e["first"], e["first"] + e["size"])
        yx_ref[at, :] = yx_ref[at, :] + sum_ref[pl.ds(e["base"], e["size"]), :].astype(F32)
    for h in range(2):
        v = yx_ref[h * T : (h + 1) * T, :] * root[h : h + 1, :]
        gf_ref[h * T : (h + 1) * T, :] = v.T.astype(BF16)
    return [plan]


COPIES = 242
ROW_NODES = PIECE * NZ * 2
COL_NODES = PIECE * NX * NY


def body(
    feat_ref, deg_ref, weight_ref, bias_ref, cot_ref, rows_ref, cols_ref, count_ref, codes_ref,
    hid_ref, gf_ref, gw_ref, gb_ref,
    xg_ref, masks_ref, tab_ref, at_ref, b_ref, pre_ref, rp_ref, racc_ref, cs_ref, zs_ref, gt_ref, cp_ref, cacc_ref,
    sum_ref, gsum_ref, gl_ref, g1_ref, gz_ref, g2_ref, g3_ref, g3x_ref, g4_ref, yx_ref,
    tab_s, tab_sem, send_sem, recv_sem,
):
    me = Place(send_sem, recv_sem)
    met = me.enter(
        [me.at_xy(o, 0) for o in (1, 2, 3)]
        + [me.at_xy(0, o) for o in (1, 2, -2, -1)]
        + [me.at_z(o) for o in (1, 2, -2, -1)]
        + [me.other]
    )
    root = lax.rsqrt(deg_ref[...].astype(F32))
    tab_ref[...] = jnp.zeros_like(tab_ref)
    plans = gather_part(
        me, root, met, feat_ref, rows_ref, cols_ref, count_ref, codes_ref, xg_ref, masks_ref, tab_ref, at_ref, b_ref
    )
    moved = pltpu.make_async_copy(tab_ref, tab_s, tab_sem)
    moved.start()
    moved.wait()
    form = product_part(True, tab_s, masks_ref, xg_ref, rp_ref, pre_ref)
    plans += dense_part(
        me, root, form, rp_ref, weight_ref, bias_ref, cot_ref, hid_ref, gt_ref, gsum_ref,
        racc_ref, cs_ref, zs_ref, gl_ref, g1_ref, gz_ref, g2_ref, g3x_ref,
    )
    form = product_part(False, tab_s, masks_ref, gt_ref, cp_ref, pre_ref)
    plans += scatter_part(
        me, root, form, cp_ref, gsum_ref, gf_ref, gw_ref, gb_ref, cacc_ref, sum_ref, g3_ref, g4_ref, yx_ref
    )
    for plan in plans:
        plan.drain()


def hand_over(*refs):
    for given, out in zip(refs[:4], refs[4:]):
        out[...] = given[...]


def local(features, degree, weight, bias, cotangent, tile_rows, tile_cols, tile_count, tile_codes):
    vmem = pl.BlockSpec(memory_space=pltpu.VMEM)
    smem = pl.BlockSpec(memory_space=pltpu.SMEM)
    hidden, grad_features, grad_weight, grad_bias = pl.pallas_call(
        body,
        out_shape=(
            jax.ShapeDtypeStruct((PIECE, T), BF16),
            jax.ShapeDtypeStruct((PIECE, T), BF16),
            jax.ShapeDtypeStruct((T, T), F32),
            jax.ShapeDtypeStruct((1, T), F32),
        ),
        in_specs=[vmem] * 7 + [smem, vmem],
        out_specs=(vmem,) * 4,
        scratch_shapes=[
            pltpu.VMEM((COL_NODES, T), BF16),
            pltpu.VMEM((SLOTS * T, T), BF16),
            pltpu.VMEM((16, T), I32),
            pltpu.VMEM((T, SLOTS), F32),
            pltpu.VMEM((SLOTS, T), F32),
            pltpu.VMEM((SLOTS * T, T), F32),
            pltpu.VMEM((ROW_NODES, T), BF16),
            pltpu.VMEM((ROW_NODES, T), BF16),
            pltpu.VMEM((PIECE * NZ, T), BF16),
            pltpu.VMEM((PIECE * (NZ - 1), T), BF16),
            pltpu.VMEM((ROW_NODES, T), BF16),
            pltpu.VMEM((COL_NODES, T), BF16),
            pltpu.VMEM((COL_NODES, T), BF16),
            pltpu.VMEM((COL_NODES - PIECE, T), BF16),
            pltpu.VMEM((16, T), F32),
            pltpu.VMEM((144, T), F32),
            pltpu.VMEM((72, T), F32),
            pltpu.VMEM((16 * NY, T), F32),
            pltpu.VMEM((16 * NY, T), F32),
            pltpu.VMEM((16 * NZ, T), F32),
            pltpu.VMEM((16 * NX, T), F32),
            pltpu.VMEM((T, T), F32),
            pltpu.VMEM((PIECE, T), F32),
            pltpu.SMEM((16, T), I32),
            pltpu.SemaphoreType.DMA,
            pltpu.SemaphoreType.DMA((COPIES,)),
            pltpu.SemaphoreType.DMA((COPIES,)),
        ],
        compiler_params=pltpu.CompilerParams(collective_id=0, has_side_effects=True),
        name="layer",
    )(
        features,
        degree.reshape(2, T),
        weight,
        bias.reshape(1, T),
        cotangent,
        tile_rows.reshape(1, SLOTS),
        tile_cols.reshape(1, SLOTS),
        tile_count.reshape(1, 1),
        tile_codes.reshape(SLOTS, 2 * T),
    )
    hidden, grad_features, grad_weight, grad_bias = pl.pallas_call(
        hand_over,
        out_shape=tuple(jax.ShapeDtypeStruct(v.shape, v.dtype) for v in (hidden, grad_features, grad_weight, grad_bias)),
        in_specs=[vmem] * 4,
        out_specs=(vmem,) * 4,
        name="hand_over",
    )(hidden, grad_features, grad_weight, grad_bias)
    return hidden, grad_features, grad_weight, grad_bias.reshape(T)


def solution(mesh):
    placed = (
        P(("row", "col"), None),
        P(("row", "col")),
        P(),
        P(),
        P(("row", "col"), None),
        P("row", "col", None),
        P("row", "col", None),
        P("row", "col", None),
        P("row", "col", None, None),
    )
    return jax.shard_map(
        local,
        mesh=mesh,
        in_specs=placed,
        out_specs=(P(("row", "col"), None), P(("row", "col"), None), P(), P()),
        check_vma=False,
    )
```
